32 devices in a mesh: groups: 2 (over x), tile: 16 (over z, y, core).
Axes of the slice: x: 2, y: 2, z: 4, core: 2. Of those that a mesh axis runs over, the one named last changes fastest.
Arguments:
- frame_one: bfloat16 [256, 128, 128], P(('groups', 'tile')), parts along dimension 0, may hold values from -6 to 6
- frame_two: bfloat16 [256, 128, 128], P(('groups', 'tile')), parts along dimension 0, may hold values from -6 to 6
- conv_weight: bfloat16 [3, 3, 128, 256], replicated, may hold values from -0.1875 to 0.1875
- partners: int32 [32, 4], P(('groups', 'tile')), parts along dimension 0, may hold values from 0 to 15, as said below
- counts: int32 [32], P(('groups', 'tile')), parts along dimension 0, may hold values from 3 to 4
- targets: int32 [256, 128], P(('groups', 'tile')), parts along dimension 0, may hold values from 0 to 4095, as said below
Outputs:
- grad_one: bfloat16 [256, 128, 128], P(('groups', 'tile')), parts along dimension 0
- grad_two: bfloat16 [256, 128, 128], P(('groups', 'tile')), parts along dimension 0
The draws below stay inside these ranges and needn't reach their ends.
There are 2 independent parts, one for each index of `groups`. The reference program is written for one: setup_inputs(seed, part) draws one part's arguments, and reference() takes and returns one part's arrays. A program takes and returns all parts, laid end to end along the dimension named above; an argument that names none is the same for every part. Nothing has to cross between parts.
Inputs may be any that keep to these rules, and one draw needn't show every extreme that they name: `partners`: row t holds counts[t] distinct tiles within 2 of t, then copies of t. `targets`: A pixel's slot v // 1024 is below counts of its tile.
All inputs are finite; a program needn't handle non-finite values.
Results may differ from the reference program's by a relative error of at most 0.005.
Values may be sent and summed in bfloat16 or wider, within the bound.
No kernel may reach another device: no remote copies, remote signals or barrier semaphores. Data moves between devices by JAX's collectives and lax.ppermute only.
A program may use at most 64 MiB of HBM per device.

```python
import math
import jax
import jax.numpy as jnp
from jax import lax

CH = 256
CIN = 128
LEVELS = 4
TR = 8
TC = 128
RADIUS = 2
SLOTS = 4
TILES = 16
ROWS = 128
QP = 1360


def search_plan(key):
    base_key = jax.random.fold_in(key, 7)
    tile_keys = jax.random.split(base_key, TILES)
    window_size = 2 * RADIUS + 1

    def one_order(tile_key):
        return jax.random.permutation(tile_key, window_size)
    orders = jax.vmap(one_order)(tile_keys).astype(jnp.int32)
    tile_ids = jnp.arange(TILES, dtype=jnp.int32)[:, None]
    partner_all = tile_ids + orders - RADIUS
    inside = (partner_all >= 0) & (partner_all < TILES)
    ranking = jnp.where(inside, 0, window_size) + jnp.arange(window_size, dtype=jnp.int32)[None, :]
    picked = jnp.argsort(ranking, axis=1)[:, :SLOTS]
    chosen = jnp.take_along_axis(partner_all, picked, axis=1)
    inside_count = jnp.sum(inside.astype(jnp.int32), axis=1)
    wanted = jax.random.randint(jax.random.fold_in(key, 5), (TILES,), RADIUS + 1, SLOTS + 1).astype(jnp.int32)
    count_all = jnp.minimum(jnp.minimum(inside_count, wanted), SLOTS).astype(jnp.int32)
    count_all = count_all.at[TILES // 2].set(SLOTS)
    usable = jnp.arange(SLOTS, dtype=jnp.int32)[None, :] < count_all[:, None]
    partner_list = jnp.where(usable, chosen, tile_ids).astype(jnp.int32)
    return (partner_list, count_all.astype(jnp.int32))


def draw_partners(key, part):
    partner_list, count_all = search_plan(key)
    return partner_list


def draw_counts(key, part):
    partner_list, count_all = search_plan(key)
    return count_all


def draw_targets(key, part):
    partner_list, count_all = search_plan(key)
    pixels = TR * TC
    slot_raw = jax.random.randint(jax.random.fold_in(key, 11), (TILES, pixels), 0, 1 << 20)
    slot_ids = slot_raw % count_all[:, None]
    pixel_ids = jax.random.randint(jax.random.fold_in(key, 13), (TILES, pixels), 0, pixels)
    values = (slot_ids * pixels + pixel_ids).astype(jnp.int32)
    middle = TILES // 2
    values = values.at[middle, pixels - 1].set((SLOTS - 1) * pixels + pixels - 1)
    values = values.at[0, 0].set(0)
    return values.reshape(TILES * TR, TC).astype(jnp.int32)


def shard_levels(key, extent, cuts, low, largest):
    def one(axis_at, parts):
        heights = jax.random.uniform(jax.random.fold_in(jax.random.fold_in(key, 6), axis_at), (parts,), jnp.float32, low / len(cuts), largest / len(cuts))
        return jnp.repeat(jnp.exp(heights), extent[axis_at] // parts).reshape((-1,) + (1,) * (len(extent) - axis_at - 1))

    gain = one(*cuts[0])
    for cut in cuts[1:]:
        gain = gain * one(*cut)
    return gain


def gaussian(key, dims, spread, most, shards=(), kind=jnp.bfloat16):
    values = jax.random.normal(key, dims, jnp.float32) * spread
    if len(shards) > 0:
        values = shard_levels(key, dims, shards, -0.22, 0.18) * values
    return jnp.clip(values, min=-most, max=most).astype(kind)


def setup_inputs(seed: int = 0, part: int = 0) -> dict:
    key_list = jax.random.split(jax.random.key(seed), 7)
    part_keys = jax.random.split(jax.random.fold_in(key_list[6], part), 7)
    frame_one = gaussian(part_keys[0], (ROWS, TC, CIN), 1.0, 6.0, ((0, 16),))
    frame_two = gaussian(part_keys[1], (ROWS, TC, CIN), 1.0, 6.0, ((0, 16),))
    conv_weight = gaussian(key_list[2], (3, 3, CIN, CH), (9 * CIN) ** -0.5, 0.1875)
    partners = draw_partners(jax.random.fold_in(jax.random.fold_in(key_list[6], part), 71), part)
    counts = draw_counts(jax.random.fold_in(jax.random.fold_in(key_list[6], part), 71), part)
    targets = draw_targets(jax.random.fold_in(jax.random.fold_in(key_list[6], part), 71), part)
    return dict(frame_one=frame_one, frame_two=frame_two, conv_weight=conv_weight, partners=partners, counts=counts, targets=targets)


score_shift = 2.0

def conv_forward(picture, kernel):
    num_rows, num_cols = (picture.shape[0], picture.shape[1])
    padded = jnp.pad(picture, ((1, 1), (1, 1), (0, 0))).astype(jnp.float32)
    summed = jnp.zeros((num_rows, num_cols, kernel.shape[3]), jnp.float32)
    for row_tap in range(3):
        for col_tap in range(3):
            window = padded[row_tap:row_tap + num_rows, col_tap:col_tap + num_cols]
            summed = summed + jnp.einsum('rci,io->rco', window, kernel[row_tap, col_tap].astype(jnp.float32))
    return summed

def conv_backward(gradient, kernel):
    num_rows, num_cols = (gradient.shape[0], gradient.shape[1])
    padded = jnp.pad(gradient, ((1, 1), (1, 1), (0, 0))).astype(jnp.float32)
    summed = jnp.zeros((num_rows, num_cols, kernel.shape[2]), jnp.float32)
    for row_tap in range(3):
        for col_tap in range(3):
            window = padded[2 - row_tap:2 - row_tap + num_rows, 2 - col_tap:2 - col_tap + num_cols]
            summed = summed + jnp.einsum('rco,io->rci', window, kernel[row_tap, col_tap].astype(jnp.float32))
    return summed

def pool_levels(features):
    num_rows, num_cols, channels = features.shape
    widened = features.astype(jnp.float32)
    stacked = []
    for level_idx in range(LEVELS):
        stride = 2 ** level_idx
        pooled = widened.reshape(num_rows // stride, stride, num_cols // stride, stride, channels).mean(axis=(1, 3))
        stacked.append(pooled.reshape(-1, channels))
    return jnp.concatenate(stacked, 0).astype(jnp.bfloat16)

def unpool_levels(summed, num_rows, num_cols):
    channels = summed.shape[1]
    result = jnp.zeros((num_rows, num_cols, channels), jnp.float32)
    offset = 0
    for level_idx in range(LEVELS):
        stride = 2 ** level_idx
        cells = num_rows // stride * (num_cols // stride)
        piece = summed[offset:offset + cells].reshape(num_rows // stride, 1, num_cols // stride, 1, channels)
        piece = jnp.broadcast_to(piece, (num_rows // stride, stride, num_cols // stride, stride, channels))
        result = result + piece.reshape(num_rows, num_cols, channels) / float(stride * stride)
        offset += cells
    return result.reshape(num_rows * num_cols, channels)

def column_scales(num_rows, num_cols, channels):
    pieces = []
    for level_idx in range(LEVELS):
        stride = 2 ** level_idx
        cells = num_rows // stride * (num_cols // stride)
        pieces.append(jnp.full((cells,), 2.0 ** level_idx / math.sqrt(channels), jnp.float32))
    return jnp.concatenate(pieces, 0)

def label_columns(target_row, num_rows, num_cols):
    pixels = num_rows * num_cols
    slot_ids = target_row // pixels
    inside = target_row % pixels
    row_ids = inside // num_cols
    col_ids = inside % num_cols
    columns = []
    offset = 0
    for level_idx in range(LEVELS):
        stride = 2 ** level_idx
        columns.append(offset + row_ids // stride * (num_cols // stride) + col_ids // stride)
        offset += num_rows // stride * (num_cols // stride)
    return (slot_ids, jnp.stack(columns, 1).astype(jnp.int32))

def slot_gradient(scores_raw, scales, columns, is_slot, usable):
    scores = scores_raw * scales[None, :]
    positions = jnp.arange(scales.shape[0], dtype=jnp.int32)
    matched = jnp.zeros(scores.shape, jnp.float32)
    for level_idx in range(LEVELS):
        matched = matched + (positions[None, :] == columns[:, level_idx:level_idx + 1]).astype(jnp.float32)
    matched = matched * is_slot[:, None]
    return (scales[None, :] * (jax.nn.sigmoid(scores - score_shift) - matched) * usable).astype(jnp.bfloat16)

def reference(frame_one, frame_two, conv_weight, partners, counts, targets):
    feat_one = conv_forward(frame_one, conv_weight).astype(jnp.bfloat16)
    feat_two = conv_forward(frame_two, conv_weight).astype(jnp.bfloat16)
    pixels = TR * TC
    tiles_one = feat_one.reshape(TILES, pixels, CH)
    pyramid = lax.map(pool_levels, feat_two.reshape(TILES, TR, TC, CH))
    scales = column_scales(TR, TC, CH)
    tile_targets = targets.reshape(TILES, pixels)

    def per_tile(carry, inputs):
        features, partner_row, count_here, target_row = inputs
        slot_ids, columns = label_columns(target_row, TR, TC)
        grad_rows = jnp.zeros((pixels, CH), jnp.float32)
        for slot_idx in range(SLOTS):
            chosen = pyramid[partner_row[slot_idx]]
            scores_raw = jnp.dot(features, chosen.T, preferred_element_type=jnp.float32)
            usable = (slot_idx < count_here).astype(jnp.float32)
            is_slot = (slot_ids == slot_idx).astype(jnp.float32)
            dscore = slot_gradient(scores_raw, scales, columns, is_slot, usable)
            grad_rows = grad_rows + jnp.dot(dscore, chosen, preferred_element_type=jnp.float32)
            level_grad = jnp.dot(dscore.T, features, preferred_element_type=jnp.float32)
            carry = carry.at[partner_row[slot_idx]].add(level_grad)
        return (carry, grad_rows.astype(jnp.bfloat16))
    start_sum = jnp.zeros((TILES, QP, CH), jnp.float32)
    level_sum, grad_tiles = lax.scan(per_tile, start_sum, (tiles_one, partners, counts, tile_targets))

    def unpool_tile(summed):
        return unpool_levels(summed, TR, TC)
    grad_two_tiles = lax.map(unpool_tile, level_sum).astype(jnp.bfloat16)
    grad_feat_one = grad_tiles.reshape(ROWS, TC, CH)
    grad_feat_two = grad_two_tiles.reshape(ROWS, TC, CH)
    grad_one = conv_backward(grad_feat_one, conv_weight).astype(jnp.bfloat16)
    grad_two = conv_backward(grad_feat_two, conv_weight).astype(jnp.bfloat16)
    return (grad_one, grad_two)
```

```python
import functools

import jax
import jax.numpy as jnp
import numpy as np
from jax import lax
from jax.experimental import pallas as pl
from jax.experimental.pallas import tpu as pltpu
from jax.sharding import PartitionSpec as P

LEVELS = 4
RADIUS = 2
SLOTS = 4
TR = 8
TC = 128
PIX = TR * TC
CIN = 128
CH = 256
POOLED = PIX // 4 + PIX // 16 + PIX // 64
PAD = 384
CELLS = PIX + PAD
WIN = 2 * RADIUS * TR + TR + 2

NN = (((1,), (0,)), ((), ()))
NT = (((1,), (1,)), ((), ()))
TN = (((0,), (0,)), ((), ()))


def matmul(a, b, dims):
    return lax.dot_general(a, b, dims, preferred_element_type=jnp.float32)


def routes(count):
    side = [1 - 2 * (i % 2) for i in range(count)]

    def keep(pairs):
        return [(a, b) for a, b in pairs if 0 <= b < count]

    return dict(
        swap=[(i, i + side[i]) for i in range(count)],
        ahead=keep((i, i + 2 * side[i]) for i in range(count)),
        behind=keep((i, i - 2 * side[i]) for i in range(count)),
        far=keep((i, i - 3 * side[i]) for i in range(count)),
    )


def shifted(block):
    n = block.shape[0]
    column = lax.broadcasted_iota(jnp.int32, block.shape, 0)
    down = jnp.where(column == 0, 0.0, pltpu.roll(block, 1, 0))
    up = jnp.where(column == n - 1, 0.0, pltpu.roll(block, n - 1, 0))
    return down, up


def spread_columns(source, row, target, at):
    middle = source[row]
    down, up = shifted(middle.astype(jnp.float32))
    where = pl.ds(pl.multiple_of(at * TC, TC), TC)
    target[where, 0:CIN] = down.astype(jnp.bfloat16)
    target[where, CIN : 2 * CIN] = middle
    target[where, 2 * CIN : 3 * CIN] = up.astype(jnp.bfloat16)


def convolve(spread, at, weight):
    parts = [
        spread[pl.ds(pl.multiple_of((at + a) * TC, TC), PIX), :] for a in range(3)
    ]
    total = matmul(jnp.concatenate(parts, 1), weight[...], NN)
    return total.astype(jnp.bfloat16)


def convolve_back(gradient, weight_back, moved, total, at):
    for r in range(TR):
        block = gradient[r * TC : (r + 1) * TC, :]
        down, up = shifted(block)
        rows = slice(r * TC, (r + 1) * TC)
        moved[rows, 0:CH] = up.astype(jnp.bfloat16)
        moved[rows, CH : 2 * CH] = block.astype(jnp.bfloat16)
        moved[rows, 2 * CH : 3 * CH] = down.astype(jnp.bfloat16)
    for a in range(3):
        part = matmul(moved[...], weight_back[a * CIN : (a + 1) * CIN, :], NT)
        where = pl.ds(pl.multiple_of((at + a) * TC, TC), PIX)
        total[where, :] += part


def pool_matrix():
    cell = lax.broadcasted_iota(jnp.int32, (PAD, PIX), 0)
    pixel = lax.broadcasted_iota(jnp.int32, (PAD, PIX), 1)
    row, column = pixel // TC, pixel % TC
    offset = 0
    inside = jnp.zeros((PAD, PIX), jnp.bool_)
    for level in range(1, LEVELS):
        cells = PIX >> (2 * level)
        own = offset + (row >> level) * (TC >> level) + (column >> level)
        inside = inside | ((cell >= offset) & (cell < offset + cells) & (cell == own))
        offset += cells
    return jnp.where(inside, 1.0, 0.0).astype(jnp.bfloat16)


def per_level(values, fill):
    cell = lax.broadcasted_iota(jnp.int32, (PAD, 1), 0)
    result = jnp.full((PAD, 1), fill, jnp.float32)
    offset = 0
    for level in range(1, LEVELS):
        result = jnp.where(cell >= offset, values[level], result)
        offset += PIX >> (2 * level)
    return jnp.where(cell >= offset, fill, result)


def work_kernel(
    plan,
    own_one,
    own_two,
    near,
    direct,
    far,
    from_sibling,
    weight,
    labels,
    to_sibling,
    ahead,
    behind,
    far_out,
    sum_one,
    sum_two,
    window,
    spread_two,
    window_one,
    spread_one,
    weight_back,
    pool,
    feat_one,
    pyramid,
    dscore,
    level_grad,
    grad_rows,
    moved,
    total_two,
    total_one,
):
    side = plan[5]
    count = plan[4]

    def at(offset):
        return 1 + TR * (offset + RADIUS)

    def edge(sign):
        return jnp.where(sign > 0, WIN - 1, 0)

    for r in range(TR):
        window[at(0) + r] = own_two[r]
        window[at(2 * side) + r] = near[r]
        window[at(-2 * side) + r] = direct[r]
        window[at(side) + r] = from_sibling[r]
        window[at(-side) + r] = from_sibling[TR + r]
        window_one[1 + r] = own_one[r]
    window[edge(side)] = from_sibling[2 * TR + 2]
    window[edge(-side)] = far[0]
    window_one[jnp.where(side > 0, TR + 1, 0)] = from_sibling[2 * TR + 1]
    window_one[jnp.where(side > 0, 0, TR + 1)] = from_sibling[2 * TR]

    def spread(r, carry):
        spread_columns(window, r, spread_two, r)
        return carry

    lax.fori_loop(0, WIN, spread, 0)
    for r in range(TR + 2):
        spread_columns(window_one, r, spread_one, r)
    for a in range(3):
        for b in range(3):
            weight_back[a * CIN : (a + 1) * CIN, b * CH : (b + 1) * CH] = weight[
                (3 * a + b) * CIN : (3 * a + b + 1) * CIN, :
            ]
    pool[...] = pool_matrix()
    feat_one[...] = convolve(spread_one, 0, weight)
    grad_rows[...] = jnp.zeros_like(grad_rows)
    total_two[...] = jnp.zeros_like(total_two)
    total_one[...] = jnp.zeros_like(total_one)

    def slot(k, carry):
        @pl.when(k < count)
        def _():
            first = TR * (plan[k] + RADIUS)
            feat_two = convolve(spread_two, first, weight)
            pyramid[0:PIX, :] = feat_two * jnp.bfloat16(2.0**-5)
            means = matmul(pool[...], feat_two, NN) * per_level(
                [4.0**-level for level in range(LEVELS)], 0.0
            )
            scale = per_level([2.0 ** (level - 5) for level in range(LEVELS)], 0.0)
            pyramid[PIX:CELLS, :] = (
                means.astype(jnp.bfloat16).astype(jnp.float32) * scale
            ).astype(jnp.bfloat16)
            features = feat_one[...]
            here = labels[4:5, :] == k
            columns = [jnp.where(here, labels[n : n + 1, :], -1) for n in range(LEVELS)]
            for start in range(0, CELLS, 256):
                size = min(256, CELLS - start)
                half_score = matmul(pyramid[start : start + size, :], features, NT)
                position = lax.broadcasted_iota(jnp.int32, half_score.shape, 0) + start
                if start < PIX:
                    hit = position == columns[0]
                elif start < PIX + PIX // 4:
                    hit = position == columns[1]
                else:
                    hit = (position == columns[2]) | (position == columns[3])
                value = jnp.tanh(half_score - 1.0) + jnp.where(hit, -1.0, 1.0)
                dscore[start : start + size, :] = value.astype(jnp.bfloat16)
            level_grad[...] = matmul(dscore[...], features, NN)
            grad_rows[...] += matmul(dscore[...], pyramid[...], TN)
            coarse = level_grad[PIX:CELLS, :] * per_level(
                [2.0 ** (-level - 5) for level in range(LEVELS)], 0.0
            )
            high = coarse.astype(jnp.bfloat16)
            low = (coarse - high.astype(jnp.float32)).astype(jnp.bfloat16)
            gradient = level_grad[0:PIX, :] * 2.0**-5
            gradient = gradient + matmul(pool[...], high, TN)
            gradient = gradient + matmul(pool[...], low, TN)
            convolve_back(gradient, weight_back, moved, total_two, first)

        return carry

    lax.fori_loop(0, SLOTS, slot, 0)
    convolve_back(grad_rows[...], weight_back, moved, total_one, 0)

    def rows(total, row, size=1):
        return total[pl.ds(pl.multiple_of(row * TC, TC), size * TC), :].reshape(size, TC, CIN)

    to_sibling[0:TR] = rows(total_two, at(side), TR).astype(jnp.bfloat16)
    to_sibling[TR : 2 * TR] = rows(total_two, at(-side), TR).astype(jnp.bfloat16)
    to_sibling[2 * TR : 2 * TR + 1] = rows(total_two, edge(side)).astype(jnp.bfloat16)
    to_sibling[2 * TR + 1 : 2 * TR + 2] = rows(
        total_one, jnp.where(side > 0, TR + 1, 0)
    ).astype(jnp.bfloat16)
    to_sibling[2 * TR + 2 : 2 * TR + 3] = rows(
        total_one, jnp.where(side > 0, 0, TR + 1)
    ).astype(jnp.bfloat16)
    ahead[...] = rows(total_two, at(2 * side), TR)
    behind[...] = rows(total_two, at(-2 * side), TR)
    far_out[...] = rows(total_two, edge(-side)).astype(jnp.bfloat16)
    sum_two[...] = rows(total_two, at(0), TR)
    sum_one[...] = rows(total_one, 1, TR)


def join_kernel(plan, ahead, behind, from_sibling, ahead_out, behind_out, held):
    side = plan[5]
    for r in range(TR):
        ahead_out[r] = (ahead[r] + from_sibling[TR + r].astype(jnp.float32)).astype(jnp.bfloat16)
    ahead_out[TR] = from_sibling[2 * TR + 2]
    held[...] = behind[...]
    row = jnp.where(side > 0, TR - 1, 0)
    held[row] = held[row] + from_sibling[2 * TR].astype(jnp.float32)
    behind_out[...] = held[...].astype(jnp.bfloat16)


def final_kernel(plan, sum_one, sum_two, from_sibling, ahead, behind, far, one, two, held_one, held_two):
    side = plan[5]
    facing = jnp.where(side > 0, TR - 1, 0)
    outer = jnp.where(side > 0, 0, TR - 1)
    held_one[...] = sum_one[...]
    held_one[facing] = held_one[facing] + from_sibling[2 * TR + 1].astype(jnp.float32)
    held_one[outer] = held_one[outer] + ahead[TR].astype(jnp.float32)
    one[...] = held_one[...].astype(jnp.bfloat16)
    for r in range(TR):
        held_two[r] = (
            sum_two[r]
            + from_sibling[r].astype(jnp.float32)
            + ahead[r].astype(jnp.float32)
            + behind[r].astype(jnp.float32)
        )
    held_two[outer] = held_two[outer] + far[0].astype(jnp.float32)
    two[...] = held_two[...].astype(jnp.bfloat16)


def call(kernel, outs, scratch, args, name):
    smem = pl.BlockSpec(memory_space=pltpu.SMEM)
    vmem = pl.BlockSpec(memory_space=pltpu.VMEM)
    return pl.pallas_call(
        kernel,
        in_specs=[smem] + [vmem] * (len(args) - 1),
        out_specs=[vmem] * len(outs),
        out_shape=[jax.ShapeDtypeStruct(*out) for out in outs],
        scratch_shapes=[pltpu.VMEM(*item) for item in scratch],
        compiler_params=pltpu.CompilerParams(vmem_limit_bytes=56 << 20),
        name=name,
    )(*args)


def label_rows(targets):
    value = targets.reshape(PIX)
    inside = value % PIX
    row, column = inside // TC, inside % TC
    rows = []
    offset = 0
    for level in range(LEVELS):
        rows.append(offset + (row >> level) * (TC >> level) + (column >> level))
        offset += PIX >> (2 * level)
    rows.append(value // PIX)
    rows += [rows[-1]] * 3
    return jnp.stack(rows).astype(jnp.int32)


def on_device(frame_one, frame_two, conv_weight, partners, counts, targets):
    route = routes(lax.axis_size("tile"))
    index = lax.axis_index("tile")
    side = 1 - 2 * (index % 2)
    f32, bf16 = jnp.float32, jnp.bfloat16

    def send(block, name):
        return lax.ppermute(block, "tile", route[name])

    def row_of(frame, first):
        return lax.dynamic_slice_in_dim(frame, jnp.where(first, 0, TR - 1), 1, 0)

    plan = jnp.concatenate(
        [partners[0] - index, counts, side[None], jnp.zeros((2,), jnp.int32)]
    ).astype(jnp.int32)
    labels = label_rows(targets)
    weight = conv_weight.reshape(9 * CIN, CH)
    outward = row_of(frame_one, side > 0)
    near = send(jnp.concatenate([frame_two, outward]), "behind")
    direct = send(frame_two, "ahead")
    far = send(row_of(frame_two, side > 0), "far")
    inward = row_of(frame_one, side < 0)
    payload = jnp.concatenate([frame_two, near, inward, row_of(direct, side < 0)])
    from_sibling = send(payload, "swap")

    tile = (TR, TC, CIN)
    pack = (2 * TR + 3, TC, CIN)
    to_sibling, ahead, behind, far_out, sum_one, sum_two = call(
        work_kernel,
        [(pack, bf16), (tile, f32), (tile, f32), ((1, TC, CIN), bf16), (tile, f32), (tile, f32)],
        [
            ((WIN, TC, CIN), bf16),
            ((WIN * TC, 3 * CIN), bf16),
            ((TR + 2, TC, CIN), bf16),
            (((TR + 2) * TC, 3 * CIN), bf16),
            ((3 * CIN, 3 * CH), bf16),
            ((PAD, PIX), bf16),
            ((PIX, CH), bf16),
            ((CELLS, CH), bf16),
            ((CELLS, PIX), bf16),
            ((CELLS, CH), f32),
            ((PIX, CH), f32),
            ((PIX, 3 * CH), bf16),
            ((WIN * TC, CIN), f32),
            (((TR + 2) * TC, CIN), f32),
        ],
        [plan, frame_one, frame_two, near, direct, far, from_sibling, weight, labels],
        "work",
    )
    back_sibling = send(to_sibling, "swap")
    ahead_out, behind_out = call(
        join_kernel,
        [((TR + 1, TC, CIN), bf16), (tile, bf16)],
        [(tile, f32)],
        [plan, ahead, behind, back_sibling],
        "join",
    )
    back_ahead = send(ahead_out, "ahead")
    back_behind = send(behind_out, "behind")
    back_far = send(far_out, "far")
    return call(
        final_kernel,
        [(tile, bf16), (tile, bf16)],
        [(tile, f32), (tile, f32)],
        [plan, sum_one, sum_two, back_sibling, back_ahead, back_behind, back_far],
        "final",
    )


def solution(mesh):
    return jax.shard_map(
        on_device,
        mesh=mesh,
        in_specs=(
            P(("groups", "tile"), None, None),
            P(("groups", "tile"), None, None),
            P(),
            P(("groups", "tile"), None),
            P(("groups", "tile")),
            P(("groups", "tile"), None),
        ),
        out_specs=(P(("groups", "tile"), None, None), P(("groups", "tile"), None, None)),
        check_vma=False,
    )
```

```python
import functools

import jax
import jax.numpy as jnp
import numpy as np
from jax import lax
from jax.experimental import pallas as pl
from jax.experimental.pallas import tpu as pltpu
from jax.sharding import PartitionSpec as P

LEVELS = 4
RADIUS = 2
SLOTS = 4
TR = 8
TC = 128
PIX = TR * TC
CIN = 128
CH = 256
POOLED = PIX // 4 + PIX // 16 + PIX // 64
PAD = 384
CELLS = PIX + PAD
LIMIT = 56
WIN = 2 * RADIUS * TR + TR + 2

NN = (((1,), (0,)), ((), ()))
NT = (((1,), (1,)), ((), ()))
TN = (((0,), (0,)), ((), ()))


def matmul(a, b, dims):
    return lax.dot_general(a, b, dims, preferred_element_type=jnp.float32)


def routes(count):
    side = [1 - 2 * (i % 2) for i in range(count)]

    def keep(pairs):
        return [(a, b) for a, b in pairs if 0 <= b < count]

    return dict(
        swap=[(i, i + side[i]) for i in range(count)],
        ahead=keep((i, i + 2 * side[i]) for i in range(count)),
        behind=keep((i, i - 2 * side[i]) for i in range(count)),
        far=keep((i, i - 3 * side[i]) for i in range(count)),
    )


def shifted(block):
    n = block.shape[0]
    column = lax.broadcasted_iota(jnp.int32, block.shape, 0)
    down = jnp.where(column == 0, 0.0, pltpu.roll(block, 1, 0))
    up = jnp.where(column == n - 1, 0.0, pltpu.roll(block, n - 1, 0))
    return down, up


def spread_columns(source, row, target, at):
    middle = source[row]
    down, up = shifted(middle.astype(jnp.float32))
    where = pl.ds(pl.multiple_of(at * TC, TC), TC)
    target[where, 0:CIN] = down.astype(jnp.bfloat16)
    target[where, CIN : 2 * CIN] = middle
    target[where, 2 * CIN : 3 * CIN] = up.astype(jnp.bfloat16)


def convolve(spread, at, weight):
    parts = [
        spread[pl.ds(pl.multiple_of((at + a) * TC, TC), PIX), :] for a in range(3)
    ]
    total = matmul(jnp.concatenate(parts, 1), weight[...], NN)
    return total.astype(jnp.bfloat16)


def convolve_back(gradient, weight_back, moved, total, at):
    for r in range(TR):
        block = gradient[r * TC : (r + 1) * TC, :]
        down, up = shifted(block)
        rows = slice(r * TC, (r + 1) * TC)
        moved[rows, 0:CH] = up.astype(jnp.bfloat16)
        moved[rows, CH : 2 * CH] = block.astype(jnp.bfloat16)
        moved[rows, 2 * CH : 3 * CH] = down.astype(jnp.bfloat16)
    parts = matmul(moved[...], weight_back[...], NT)
    for a in range(3):
        where = pl.ds(pl.multiple_of((at + a) * TC, TC), PIX)
        total[where, :] += parts[:, a * CIN : (a + 1) * CIN]


def pool_matrix(shape, cell_axis, values):
    cell = lax.broadcasted_iota(jnp.int32, shape, cell_axis)
    pixel = lax.broadcasted_iota(jnp.int32, shape, 1 - cell_axis)
    row, column = pixel // TC, pixel % TC
    offset = 0
    result = jnp.zeros(shape, jnp.float32)
    for level in range(1, LEVELS):
        own = offset + (row >> level) * (TC >> level) + (column >> level)
        result = jnp.where(cell == own, values[level], result)
        offset += PIX >> (2 * level)
    return result.astype(jnp.bfloat16)


def per_level(values, fill):
    cell = lax.broadcasted_iota(jnp.int32, (PAD, 1), 0)
    result = jnp.full((PAD, 1), fill, jnp.float32)
    offset = 0
    for level in range(1, LEVELS):
        result = jnp.where(cell >= offset, values[level], result)
        offset += PIX >> (2 * level)
    return jnp.where(cell >= offset, fill, result)


def tables_kernel(weight, weight_back, pool, unpool):
    for a in range(3):
        for b in range(3):
            weight_back[a * CIN : (a + 1) * CIN, b * CH : (b + 1) * CH] = weight[
                (3 * a + b) * CIN : (3 * a + b + 1) * CIN, :
            ]
    pool[...] = pool_matrix((PAD, PIX), 0, [1.0] * LEVELS)
    unpool[...] = pool_matrix((PIX, PAD), 1, [2.0**-level for level in range(LEVELS)])


def work_kernel(
    plan,
    own_one,
    own_two,
    near,
    direct,
    far,
    from_sibling,
    weight,
    weight_back,
    pool,
    unpool,
    labels,
    to_sibling,
    ahead,
    behind,
    far_out,
    sum_one,
    sum_two,
    window,
    spread_two,
    window_one,
    spread_one,
    feat_one,
    pyramid,
    dscore,
    level_grad,
    grad_rows,
    moved,
    total_two,
    total_one,
):
    side = plan[5]
    count = plan[4]

    def at(offset):
        return 1 + TR * (offset + RADIUS)

    def edge(sign):
        return jnp.where(sign > 0, WIN - 1, 0)

    for r in range(TR):
        window[at(0) + r] = own_two[r]
        window[at(2 * side) + r] = near[r]
        window[at(-2 * side) + r] = direct[r]
        window[at(side) + r] = from_sibling[r]
        window[at(-side) + r] = from_sibling[TR + r]
        window_one[1 + r] = own_one[r]
    window[edge(side)] = from_sibling[2 * TR + 2]
    window[edge(-side)] = far[0]
    window_one[jnp.where(side > 0, TR + 1, 0)] = from_sibling[2 * TR + 1]
    window_one[jnp.where(side > 0, 0, TR + 1)] = from_sibling[2 * TR]

    def spread(r, carry):
        spread_columns(window, r, spread_two, r)
        return carry

    lax.fori_loop(0, WIN, spread, 0)
    for r in range(TR + 2):
        spread_columns(window_one, r, spread_one, r)
    feat_one[...] = convolve(spread_one, 0, weight)
    grad_rows[...] = jnp.zeros_like(grad_rows)
    total_two[...] = jnp.zeros_like(total_two)
    total_one[...] = jnp.zeros_like(total_one)

    def slot(k, carry):
        @pl.when(k < count)
        def _():
            first = TR * (plan[k] + RADIUS)
            feat_two = convolve(spread_two, first, weight)
            pyramid[0:PIX, :] = feat_two * jnp.bfloat16(2.0**-5)
            means = matmul(pool[...], feat_two, NN) * per_level(
                [4.0**-level for level in range(LEVELS)], 0.0
            )
            scale = per_level([2.0 ** (level - 5) for level in range(LEVELS)], 0.0)
            pyramid[PIX:CELLS, :] = (
                means.astype(jnp.bfloat16).astype(jnp.float32) * scale
            ).astype(jnp.bfloat16)
            features = feat_one[...]
            here = labels[4:5, :] == k
            columns = [jnp.where(here, labels[n : n + 1, :], -1) for n in range(LEVELS)]
            for start in range(0, CELLS, 256):
                size = min(256, CELLS - start)
                half_score = matmul(pyramid[start : start + size, :], features, NT)
                position = lax.broadcasted_iota(jnp.int32, half_score.shape, 0) + start
                if start < PIX:
                    hit = position == columns[0]
                elif start < PIX + PIX // 4:
                    hit = position == columns[1]
                else:
                    hit = (position == columns[2]) | (position == columns[3])
                value = jnp.tanh(half_score - 1.0) + jnp.where(hit, -1.0, 1.0)
                dscore[start : start + size, :] = value.astype(jnp.bfloat16)
            level_grad[...] = matmul(dscore[...], features, NN)
            grad_rows[...] += matmul(dscore[...], pyramid[...], TN)
            coarse = level_grad[PIX:CELLS, :].astype(jnp.bfloat16)
            gradient = level_grad[0:PIX, :] + matmul(unpool[...], coarse, NN)
            gradient = gradient * 2.0**-5
            convolve_back(gradient, weight_back, moved, total_two, first)

        return carry

    lax.fori_loop(0, SLOTS, slot, 0)
    convolve_back(grad_rows[...], weight_back, moved, total_one, 0)

    def rows(total, row, size=1):
        return total[pl.ds(pl.multiple_of(row * TC, TC), size * TC), :].reshape(size, TC, CIN)

    to_sibling[0:TR] = rows(total_two, at(side), TR).astype(jnp.bfloat16)
    to_sibling[TR : 2 * TR] = rows(total_two, at(-side), TR).astype(jnp.bfloat16)
    to_sibling[2 * TR : 2 * TR + 1] = rows(total_two, edge(side)).astype(jnp.bfloat16)
    to_sibling[2 * TR + 1 : 2 * TR + 2] = rows(
        total_one, jnp.where(side > 0, TR + 1, 0)
    ).astype(jnp.bfloat16)
    to_sibling[2 * TR + 2 : 2 * TR + 3] = rows(
        total_one, jnp.where(side > 0, 0, TR + 1)
    ).astype(jnp.bfloat16)
    ahead[...] = rows(total_two, at(2 * side), TR)
    behind[...] = rows(total_two, at(-2 * side), TR).astype(jnp.bfloat16)
    far_out[...] = rows(total_two, edge(-side)).astype(jnp.bfloat16)
    sum_two[...] = rows(total_two, at(0), TR)
    sum_one[...] = rows(total_one, 1, TR)


def call(kernel, outs, scratch, args, name, scalars=1, limit=LIMIT):
    smem = pl.BlockSpec(memory_space=pltpu.SMEM)
    vmem = pl.BlockSpec(memory_space=pltpu.VMEM)
    return pl.pallas_call(
        kernel,
        in_specs=[smem] * scalars + [vmem] * (len(args) - scalars),
        out_specs=[vmem] * len(outs),
        out_shape=[jax.ShapeDtypeStruct(*out) for out in outs],
        scratch_shapes=[pltpu.VMEM(*item) for item in scratch],
        compiler_params=pltpu.CompilerParams(vmem_limit_bytes=limit << 20),
        name=name,
    )(*args)


def label_rows(targets):
    value = targets.reshape(PIX)
    inside = value % PIX
    row, column = inside // TC, inside % TC
    rows = []
    offset = 0
    for level in range(LEVELS):
        rows.append(offset + (row >> level) * (TC >> level) + (column >> level))
        offset += PIX >> (2 * level)
    rows.append(value // PIX)
    rows += [rows[-1]] * 3
    return jnp.stack(rows).astype(jnp.int32)


def on_device(frame_one, frame_two, conv_weight, partners, counts, targets):
    route = routes(lax.axis_size("tile"))
    index = lax.axis_index("tile")
    side = 1 - 2 * (index % 2)
    f32, bf16 = jnp.float32, jnp.bfloat16

    def send(block, name):
        return lax.ppermute(block, "tile", route[name])

    def row_of(frame, first):
        return lax.dynamic_slice_in_dim(frame, jnp.where(first, 0, TR - 1), 1, 0)

    plan = jnp.concatenate(
        [partners[0] - index, counts, side[None], jnp.zeros((2,), jnp.int32)]
    ).astype(jnp.int32)
    labels = label_rows(targets)
    weight = conv_weight.reshape(9 * CIN, CH)
    direct = send(frame_two, "ahead")
    near_in = jnp.concatenate([frame_two, row_of(frame_one, side > 0)])
    near = send(near_in, "behind")
    tables = call(
        tables_kernel,
        [((3 * CIN, 3 * CH), bf16), ((PAD, PIX), bf16), ((PIX, PAD), bf16)],
        [],
        [weight],
        "tables",
        scalars=0,
    )
    inward = row_of(frame_one, side < 0)
    far_in, direct = lax.optimization_barrier((row_of(frame_two, side > 0), direct))
    far = send(far_in, "far")
    payload = jnp.concatenate([frame_two, near, inward, row_of(direct, side < 0)])
    payload, tables, labels, plan = lax.optimization_barrier((payload, tables, labels, plan))
    from_sibling = send(payload, "swap")

    tile = (TR, TC, CIN)
    pack = (2 * TR + 3, TC, CIN)
    to_sibling, ahead, behind, far_out, sum_one, sum_two = call(
        work_kernel,
        [(pack, bf16), (tile, f32), (tile, bf16), ((1, TC, CIN), bf16), (tile, f32), (tile, f32)],
        [
            ((WIN, TC, CIN), bf16),
            ((WIN * TC, 3 * CIN), bf16),
            ((TR + 2, TC, CIN), bf16),
            (((TR + 2) * TC, 3 * CIN), bf16),
            ((PIX, CH), bf16),
            ((CELLS, CH), bf16),
            ((CELLS, PIX), bf16),
            ((CELLS, CH), f32),
            ((PIX, CH), f32),
            ((PIX, 3 * CH), bf16),
            ((WIN * TC, CIN), f32),
            (((TR + 2) * TC, CIN), f32),
        ],
        [plan, frame_one, frame_two, near, direct, far, from_sibling, weight, *tables, labels],
        "work",
    )
    back_behind = send(behind, "behind")
    back_sibling = send(to_sibling, "swap")
    joined = (ahead + back_sibling[TR : 2 * TR].astype(f32)).astype(bf16)
    ahead_in = jnp.concatenate([joined, back_sibling[2 * TR + 2 :]])
    far_out, edge, ahead_in = lax.optimization_barrier(
        (far_out, back_sibling[2 * TR : 2 * TR + 1], ahead_in)
    )
    back_ahead = send(ahead_in, "ahead")
    back_far = send(far_out, "far")
    back_edge = send(edge, "behind")

    row = lax.broadcasted_iota(jnp.int32, (TR, 1, 1), 0)
    facing = row == jnp.where(side > 0, TR - 1, 0)
    outer = row == jnp.where(side > 0, 0, TR - 1)

    def place(where, block):
        return jnp.where(where, block.astype(f32), 0.0)

    grad_one = sum_one + place(facing, back_sibling[2 * TR + 1 : 2 * TR + 2])
    grad_one = grad_one + place(outer, back_ahead[TR:])
    grad_two = sum_two + back_sibling[:TR].astype(f32) + back_ahead[:TR].astype(f32)
    grad_two = grad_two + back_behind.astype(f32)
    grad_two = grad_two + place(outer, back_far) + place(facing, back_edge)
    return grad_one.astype(bf16), grad_two.astype(bf16)


def solution(mesh):
    return jax.shard_map(
        on_device,
        mesh=mesh,
        in_specs=(
            P(("groups", "tile"), None, None),
            P(("groups", "tile"), None, None),
            P(),
            P(("groups", "tile"), None),
            P(("groups", "tile")),
            P(("groups", "tile"), None),
        ),
        out_specs=(P(("groups", "tile"), None, None), P(("groups", "tile"), None, None)),
        check_vma=False,
    )
```

```python
import functools

import jax
import jax.numpy as jnp
import numpy as np
from jax import lax
from jax.experimental import pallas as pl
from jax.experimental.pallas import tpu as pltpu
from jax.sharding import PartitionSpec as P

LEVELS = 4
RADIUS = 2
SLOTS = 4
TR = 8
TC = 128
PIX = TR * TC
CIN = 128
CH = 256
POOLED = PIX // 4 + PIX // 16 + PIX // 64
PAD = 384
CELLS = PIX + PAD
LIMIT = 40
WIN = 2 * RADIUS * TR + TR + 2

NN = (((1,), (0,)), ((), ()))
NT = (((1,), (1,)), ((), ()))
TN = (((0,), (0,)), ((), ()))


def matmul(a, b, dims):
    return lax.dot_general(a, b, dims, preferred_element_type=jnp.float32)


def routes(count):
    side = [1 - 2 * (i % 2) for i in range(count)]

    def keep(pairs):
        return [(a, b) for a, b in pairs if 0 <= b < count]

    return dict(
        swap=[(i, i + side[i]) for i in range(count)],
        ahead=keep((i, i + 2 * side[i]) for i in range(count)),
        behind=keep((i, i - 2 * side[i]) for i in range(count)),
        far=keep((i, i - 3 * side[i]) for i in range(count)),
        cross=keep((i, i - side[i]) for i in range(count)),
    )


def shifted(block):
    n = block.shape[0]
    column = lax.broadcasted_iota(jnp.int32, block.shape, 0)
    down = jnp.where(column == 0, 0.0, pltpu.roll(block, 1, 0))
    up = jnp.where(column == n - 1, 0.0, pltpu.roll(block, n - 1, 0))
    return down, up


def spread_columns(source, row, target, at):
    middle = source[row]
    down, up = shifted(middle.astype(jnp.float32))
    where = pl.ds(pl.multiple_of(at * TC, TC), TC)
    target[where, 0:CIN] = down.astype(jnp.bfloat16)
    target[where, CIN : 2 * CIN] = middle
    target[where, 2 * CIN : 3 * CIN] = up.astype(jnp.bfloat16)


def convolve(spread, at, weight):
    parts = [
        spread[pl.ds(pl.multiple_of((at + a) * TC, TC), PIX), :] for a in range(3)
    ]
    total = matmul(jnp.concatenate(parts, 1), weight[...], NN)
    return total.astype(jnp.bfloat16)


def convolve_back(gradient, weight_back, moved, total, at):
    for r in range(TR):
        block = gradient[r * TC : (r + 1) * TC, :]
        down, up = shifted(block)
        rows = slice(r * TC, (r + 1) * TC)
        moved[rows, 0:CH] = up.astype(jnp.bfloat16)
        moved[rows, CH : 2 * CH] = block.astype(jnp.bfloat16)
        moved[rows, 2 * CH : 3 * CH] = down.astype(jnp.bfloat16)
    parts = matmul(moved[...], weight_back[...], NT)
    for a in range(3):
        where = pl.ds(pl.multiple_of((at + a) * TC, TC), PIX)
        total[where, :] += parts[:, a * CIN : (a + 1) * CIN]


def pool_matrix(shape, cell_axis, values):
    cell = lax.broadcasted_iota(jnp.int32, shape, cell_axis)
    pixel = lax.broadcasted_iota(jnp.int32, shape, 1 - cell_axis)
    row, column = pixel // TC, pixel % TC
    offset = 0
    result = jnp.zeros(shape, jnp.float32)
    for level in range(1, LEVELS):
        own = offset + (row >> level) * (TC >> level) + (column >> level)
        result = jnp.where(cell == own, values[level], result)
        offset += PIX >> (2 * level)
    return result.astype(jnp.bfloat16)


def per_level(values, fill):
    cell = lax.broadcasted_iota(jnp.int32, (PAD, 1), 0)
    result = jnp.full((PAD, 1), fill, jnp.float32)
    offset = 0
    for level in range(1, LEVELS):
        result = jnp.where(cell >= offset, values[level], result)
        offset += PIX >> (2 * level)
    return jnp.where(cell >= offset, fill, result)


def tables_kernel(pool, unpool):
    pool[...] = pool_matrix((PAD, PIX), 0, [1.0] * LEVELS)
    unpool[...] = pool_matrix((PIX, PAD), 1, [2.0**-level for level in range(LEVELS)])


def work_kernel(
    plan,
    own_one,
    own_two,
    near,
    direct,
    far,
    cross,
    from_sibling,
    weight,
    pool,
    unpool,
    labels,
    to_sibling_hbm,
    ahead_hbm,
    behind_hbm,
    far_hbm,
    sum_one_hbm,
    sum_two_hbm,
    to_sibling,
    ahead,
    behind,
    far_out,
    sum_one,
    sum_two,
    sems,
    weight_back,
    window,
    spread_two,
    window_one,
    spread_one,
    feat_one,
    pyramid,
    dscore,
    level_grad,
    grad_rows,
    moved,
    total_two,
    total_one,
):
    side = plan[5]
    count = plan[4]

    def at(offset):
        return 1 + TR * (offset + RADIUS)

    def edge(sign):
        return jnp.where(sign > 0, WIN - 1, 0)

    for r in range(TR):
        window[at(0) + r] = own_two[r]
        window[at(2 * side) + r] = near[r]
        window[at(-2 * side) + r] = direct[r]
        window[at(side) + r] = from_sibling[r]
        window[at(-side) + r] = from_sibling[TR + r]
        window_one[1 + r] = own_one[r]
    window[edge(side)] = from_sibling[2 * TR + 1]
    window[edge(-side)] = far[0]
    window_one[jnp.where(side > 0, TR + 1, 0)] = from_sibling[2 * TR]
    window_one[jnp.where(side > 0, 0, TR + 1)] = cross[0]

    for a in range(3):
        for b in range(3):
            weight_back[a * CIN : (a + 1) * CIN, b * CH : (b + 1) * CH] = weight[
                (3 * a + b) * CIN : (3 * a + b + 1) * CIN, :
            ]

    def spread(r, carry):
        spread_columns(window, r, spread_two, r)
        return carry

    lax.fori_loop(0, WIN, spread, 0)
    for r in range(TR + 2):
        spread_columns(window_one, r, spread_one, r)
    feat_one[...] = convolve(spread_one, 0, weight)
    grad_rows[...] = jnp.zeros_like(grad_rows)
    total_two[...] = jnp.zeros_like(total_two)
    total_one[...] = jnp.zeros_like(total_one)

    def slot(k, carry):
        @pl.when(k < count)
        def _():
            first = TR * (plan[k] + RADIUS)
            feat_two = convolve(spread_two, first, weight)
            pyramid[0:PIX, :] = feat_two * jnp.bfloat16(2.0**-5)
            means = matmul(pool[...], feat_two, NN) * per_level(
                [4.0**-level for level in range(LEVELS)], 0.0
            )
            scale = per_level([2.0 ** (level - 5) for level in range(LEVELS)], 0.0)
            pyramid[PIX:CELLS, :] = (
                means.astype(jnp.bfloat16).astype(jnp.float32) * scale
            ).astype(jnp.bfloat16)
            features = feat_one[...]
            here = labels[4:5, :] == k
            columns = [jnp.where(here, labels[n : n + 1, :], -1) for n in range(LEVELS)]
            for start in range(0, CELLS, 256):
                size = min(256, CELLS - start)
                half_score = matmul(pyramid[start : start + size, :], features, NT)
                position = lax.broadcasted_iota(jnp.int32, half_score.shape, 0) + start
                if start < PIX:
                    hit = position == columns[0]
                elif start < PIX + PIX // 4:
                    hit = position == columns[1]
                else:
                    hit = (position == columns[2]) | (position == columns[3])
                value = jnp.tanh(half_score - 1.0) + jnp.where(hit, -1.0, 1.0)
                dscore[start : start + size, :] = value.astype(jnp.bfloat16)
            level_grad[...] = matmul(dscore[...], features, NN)
            grad_rows[...] += matmul(dscore[...], pyramid[...], TN)
            coarse = level_grad[PIX:CELLS, :].astype(jnp.bfloat16)
            gradient = level_grad[0:PIX, :] + matmul(unpool[...], coarse, NN)
            gradient = gradient * 2.0**-5
            convolve_back(gradient, weight_back, moved, total_two, first)

        return carry

    lax.fori_loop(0, SLOTS, slot, 0)

    def rows(total, row, size=1):
        return total[pl.ds(pl.multiple_of(row * TC, TC), size * TC), :].reshape(size, TC, CIN)

    def out(n, block, target):
        return pltpu.make_async_copy(block, target, sems.at[n])

    behind[...] = rows(total_two, at(-2 * side), TR).astype(jnp.bfloat16)
    out(0, behind, behind_hbm).start()
    far_out[...] = rows(total_two, edge(-side)).astype(jnp.bfloat16)
    out(1, far_out, far_hbm).start()
    ahead[...] = rows(total_two, at(2 * side), TR)
    out(2, ahead, ahead_hbm).start()
    sum_two[...] = rows(total_two, at(0), TR)
    out(3, sum_two, sum_two_hbm).start()
    to_sibling[0:TR] = rows(total_two, at(side), TR).astype(jnp.bfloat16)
    to_sibling[TR : 2 * TR] = rows(total_two, at(-side), TR).astype(jnp.bfloat16)
    to_sibling[2 * TR : 2 * TR + 1] = rows(total_two, edge(side)).astype(jnp.bfloat16)
    convolve_back(grad_rows[...], weight_back, moved, total_one, 0)
    facing = jnp.where(side > 0, TR + 1, 0)
    outer = jnp.where(side > 0, 0, TR + 1)
    to_sibling[2 * TR + 1 : 2 * TR + 2] = rows(total_one, facing).astype(jnp.bfloat16)
    to_sibling[2 * TR + 2 : 2 * TR + 3] = rows(total_one, outer).astype(jnp.bfloat16)
    out(4, to_sibling, to_sibling_hbm).start()
    sum_one[...] = rows(total_one, 1, TR)
    out(5, sum_one, sum_one_hbm).start()
    out(0, behind, behind_hbm).wait()
    out(1, far_out, far_hbm).wait()
    out(2, ahead, ahead_hbm).wait()
    out(3, sum_two, sum_two_hbm).wait()
    out(4, to_sibling, to_sibling_hbm).wait()
    out(5, sum_one, sum_one_hbm).wait()


def call(kernel, outs, scratch, args, name, scalars, space):
    smem = pl.BlockSpec(memory_space=pltpu.SMEM)
    vmem = pl.BlockSpec(memory_space=pltpu.VMEM)
    return pl.pallas_call(
        kernel,
        in_specs=[smem] * scalars + [vmem] * (len(args) - scalars),
        out_specs=[pl.BlockSpec(memory_space=space)] * len(outs),
        out_shape=[jax.ShapeDtypeStruct(*out) for out in outs],
        scratch_shapes=scratch,
        compiler_params=pltpu.CompilerParams(vmem_limit_bytes=LIMIT << 20),
        name=name,
    )(*args)


def label_rows(targets):
    value = targets.reshape(PIX)
    inside = value % PIX
    row, column = inside // TC, inside % TC
    rows = []
    offset = 0
    for level in range(LEVELS):
        rows.append(offset + (row >> level) * (TC >> level) + (column >> level))
        offset += PIX >> (2 * level)
    rows.append(value // PIX)
    rows += [rows[-1]] * 3
    return jnp.stack(rows).astype(jnp.int32)


def on_device(frame_one, frame_two, conv_weight, partners, counts, targets):
    route = routes(lax.axis_size("tile"))
    index = lax.axis_index("tile")
    side = 1 - 2 * (index % 2)
    f32, bf16 = jnp.float32, jnp.bfloat16

    def send(block, name):
        return lax.ppermute(block, "tile", route[name])

    def row_of(frame, first):
        return lax.dynamic_slice_in_dim(frame, jnp.where(first, 0, TR - 1), 1, 0)

    plan = jnp.concatenate(
        [partners[0] - index, counts, side[None], jnp.zeros((2,), jnp.int32)]
    ).astype(jnp.int32)
    labels = label_rows(targets)
    weight = conv_weight.reshape(9 * CIN, CH)
    near = send(frame_two, "behind")
    direct = send(frame_two, "ahead")
    tables = call(
        tables_kernel,
        [((PAD, PIX), bf16), ((PIX, PAD), bf16)],
        [],
        [],
        "tables",
        0,
        pltpu.VMEM,
    )
    rims = row_of(frame_two, side > 0), row_of(frame_one, side > 0)
    tables, labels, plan, rims = lax.optimization_barrier((tables, labels, plan, rims))
    far = send(rims[0], "far")
    cross = send(rims[1], "cross")
    inward = row_of(frame_one, side < 0)
    inward, far, cross = lax.optimization_barrier((inward, far, cross))
    payload = jnp.concatenate([frame_two, near, inward, row_of(direct, side < 0)])
    from_sibling = send(payload, "swap")

    tile = (TR, TC, CIN)
    pack = (2 * TR + 3, TC, CIN)
    outs = [
        (pack, bf16),
        (tile, f32),
        (tile, bf16),
        ((1, TC, CIN), bf16),
        (tile, f32),
        (tile, f32),
    ]
    scratch = [
        ((3 * CIN, 3 * CH), bf16),
        ((WIN, TC, CIN), bf16),
        ((WIN * TC, 3 * CIN), bf16),
        ((TR + 2, TC, CIN), bf16),
        (((TR + 2) * TC, 3 * CIN), bf16),
        ((PIX, CH), bf16),
        ((CELLS, CH), bf16),
        ((CELLS, PIX), bf16),
        ((CELLS, CH), f32),
        ((PIX, CH), f32),
        ((PIX, 3 * CH), bf16),
        ((WIN * TC, CIN), f32),
        (((TR + 2) * TC, CIN), f32),
    ]
    to_sibling, ahead, behind, far_out, sum_one, sum_two = call(
        work_kernel,
        outs,
        [pltpu.VMEM(*out) for out in outs]
        + [pltpu.SemaphoreType.DMA((len(outs),))]
        + [pltpu.VMEM(*item) for item in scratch],
        [plan, frame_one, frame_two, near, direct, far, cross]
        + [from_sibling, weight, *tables, labels],
        "work",
        1,
        pltpu.HBM,
    )
    back_behind = send(behind, "behind")
    back_sibling = send(to_sibling, "swap")
    joined = (ahead + back_sibling[TR : 2 * TR].astype(f32)).astype(bf16)
    ahead_in = jnp.concatenate([joined, back_sibling[2 * TR + 2 :]])
    back_ahead = send(ahead_in, "ahead")
    back_far = send(far_out, "far")
    back_edge = send(back_sibling[2 * TR : 2 * TR + 1], "behind")

    row = lax.broadcasted_iota(jnp.int32, (TR, 1, 1), 0)
    facing = row == jnp.where(side > 0, TR - 1, 0)
    outer = row == jnp.where(side > 0, 0, TR - 1)

    def place(where, block):
        return jnp.where(where, block.astype(f32), 0.0)

    grad_one = sum_one + place(facing, back_sibling[2 * TR + 1 : 2 * TR + 2])
    grad_one = grad_one + place(outer, back_ahead[TR:])
    grad_two = sum_two + back_sibling[:TR].astype(f32) + back_ahead[:TR].astype(f32)
    grad_two = grad_two + back_behind.astype(f32)
    grad_two = grad_two + place(outer, back_far) + place(facing, back_edge)
    return grad_one.astype(bf16), grad_two.astype(bf16)


def solution(mesh):
    return jax.shard_map(
        on_device,
        mesh=mesh,
        in_specs=(
            P(("groups", "tile"), None, None),
            P(("groups", "tile"), None, None),
            P(),
            P(("groups", "tile"), None),
            P(("groups", "tile")),
            P(("groups", "tile"), None),
        ),
        out_specs=(P(("groups", "tile"), None, None), P(("groups", "tile"), None, None)),
        check_vma=False,
    )
```

```python
import functools

import jax
import jax.numpy as jnp
import numpy as np
from jax import lax
from jax.experimental import pallas as pl
from jax.experimental.pallas import tpu as pltpu
from jax.sharding import PartitionSpec as P

LEVELS = 4
RADIUS = 2
SLOTS = 4
TR = 8
TC = 128
PIX = TR * TC
CIN = 128
CH = 256
POOLED = PIX // 4 + PIX // 16 + PIX // 64
PAD = 384
CELLS = PIX + PAD
LIMIT = 48
WIN = 2 * RADIUS * TR + TR + 2

NN = (((1,), (0,)), ((), ()))
NT = (((1,), (1,)), ((), ()))
TN = (((0,), (0,)), ((), ()))


def matmul(a, b, dims):
    return lax.dot_general(a, b, dims, preferred_element_type=jnp.float32)


def routes(count):
    side = [1 - 2 * (i % 2) for i in range(count)]

    def keep(pairs):
        return [(a, b) for a, b in pairs if 0 <= b < count]

    return dict(
        swap=[(i, i + side[i]) for i in range(count)],
        ahead=keep((i, i + 2 * side[i]) for i in range(count)),
        behind=keep((i, i - 2 * side[i]) for i in range(count)),
        far=keep((i, i - 3 * side[i]) for i in range(count)),
        cross=keep((i, i - side[i]) for i in range(count)),
    )


def shifted(block):
    n = block.shape[0]
    column = lax.broadcasted_iota(jnp.int32, block.shape, 0)
    down = jnp.where(column == 0, 0.0, pltpu.roll(block, 1, 0))
    up = jnp.where(column == n - 1, 0.0, pltpu.roll(block, n - 1, 0))
    return down, up


def spread_columns(source, row, target, at):
    middle = source[row]
    down, up = shifted(middle.astype(jnp.float32))
    where = pl.ds(pl.multiple_of(at * TC, TC), TC)
    target[where, 0:CIN] = down.astype(jnp.bfloat16)
    target[where, CIN : 2 * CIN] = middle
    target[where, 2 * CIN : 3 * CIN] = up.astype(jnp.bfloat16)


def convolve(spread, at, weight):
    parts = [
        spread[pl.ds(pl.multiple_of((at + a) * TC, TC), PIX), :] for a in range(3)
    ]
    total = matmul(jnp.concatenate(parts, 1), weight[...], NN)
    return total.astype(jnp.bfloat16)


def convolve_back(gradient, weight_back, moved, total, at):
    for r in range(TR):
        block = gradient[r * TC : (r + 1) * TC, :]
        down, up = shifted(block)
        rows = slice(r * TC, (r + 1) * TC)
        moved[rows, 0:CH] = up.astype(jnp.bfloat16)
        moved[rows, CH : 2 * CH] = block.astype(jnp.bfloat16)
        moved[rows, 2 * CH : 3 * CH] = down.astype(jnp.bfloat16)
    parts = matmul(moved[...], weight_back[...], NT)
    for a in range(3):
        where = pl.ds(pl.multiple_of((at + a) * TC, TC), PIX)
        total[where, :] += parts[:, a * CIN : (a + 1) * CIN]


def pool_matrix(shape, cell_axis, values):
    cell = lax.broadcasted_iota(jnp.int32, shape, cell_axis)
    pixel = lax.broadcasted_iota(jnp.int32, shape, 1 - cell_axis)
    row, column = pixel // TC, pixel % TC
    offset = 0
    result = jnp.zeros(shape, jnp.float32)
    for level in range(1, LEVELS):
        own = offset + (row >> level) * (TC >> level) + (column >> level)
        result = jnp.where(cell == own, values[level], result)
        offset += PIX >> (2 * level)
    return result.astype(jnp.bfloat16)


def per_level(values, fill):
    cell = lax.broadcasted_iota(jnp.int32, (PAD, 1), 0)
    result = jnp.full((PAD, 1), fill, jnp.float32)
    offset = 0
    for level in range(1, LEVELS):
        result = jnp.where(cell >= offset, values[level], result)
        offset += PIX >> (2 * level)
    return jnp.where(cell >= offset, fill, result)


def tables_kernel(pool, unpool):
    pool[...] = pool_matrix((PAD, PIX), 0, [1.0] * LEVELS)
    unpool[...] = pool_matrix((PIX, PAD), 1, [2.0**-level for level in range(LEVELS)])


def work_kernel(
    plan,
    own_one,
    own_two,
    near,
    direct,
    far,
    cross,
    from_sibling,
    weight,
    pool,
    unpool,
    labels,
    to_sibling_hbm,
    ahead_hbm,
    behind_hbm,
    far_hbm,
    sum_one_hbm,
    sum_two_hbm,
    to_sibling,
    ahead,
    behind,
    far_out,
    sum_one,
    sum_two,
    sems,
    weight_back,
    window,
    spread_two,
    window_one,
    spread_one,
    feat_one,
    pyramid,
    dscore,
    level_grad,
    grad_rows,
    moved,
    total_two,
    total_one,
):
    side = plan[5]
    count = plan[4]

    def at(offset):
        return 1 + TR * (offset + RADIUS)

    def edge(sign):
        return jnp.where(sign > 0, WIN - 1, 0)

    for r in range(TR):
        window[at(0) + r] = own_two[r]
        window[at(2 * side) + r] = near[r]
        window[at(-2 * side) + r] = direct[r]
        window[at(side) + r] = from_sibling[r]
        window[at(-side) + r] = from_sibling[TR + r]
        window_one[1 + r] = own_one[r]
    window[edge(side)] = from_sibling[2 * TR + 1]
    window[edge(-side)] = far[0]
    window_one[jnp.where(side > 0, TR + 1, 0)] = from_sibling[2 * TR]
    window_one[jnp.where(side > 0, 0, TR + 1)] = cross[0]

    for a in range(3):
        for b in range(3):
            weight_back[a * CIN : (a + 1) * CIN, b * CH : (b + 1) * CH] = weight[
                (3 * a + b) * CIN : (3 * a + b + 1) * CIN, :
            ]

    def spread(r, carry):
        spread_columns(window, r, spread_two, r)
        return carry

    lax.fori_loop(0, WIN, spread, 0)
    for r in range(TR + 2):
        spread_columns(window_one, r, spread_one, r)
    feat_one[...] = convolve(spread_one, 0, weight)
    grad_rows[...] = jnp.zeros_like(grad_rows)
    total_two[...] = jnp.zeros_like(total_two)
    total_one[...] = jnp.zeros_like(total_one)

    def slot(k, carry):
        @pl.when(k < count)
        def _():
            first = TR * (plan[k] + RADIUS)
            feat_two = convolve(spread_two, first, weight)
            pyramid[0:PIX, :] = feat_two * jnp.bfloat16(2.0**-5)
            means = matmul(pool[...], feat_two, NN) * per_level(
                [4.0**-level for level in range(LEVELS)], 0.0
            )
            scale = per_level([2.0 ** (level - 5) for level in range(LEVELS)], 0.0)
            pyramid[PIX:CELLS, :] = (
                means.astype(jnp.bfloat16).astype(jnp.float32) * scale
            ).astype(jnp.bfloat16)
            features = feat_one[...]
            here = labels[4:5, :] == k
            columns = [jnp.where(here, labels[n : n + 1, :], -1) for n in range(LEVELS)]
            for start in range(0, CELLS, 256):
                size = min(256, CELLS - start)
                half_score = matmul(pyramid[start : start + size, :], features, NT)
                position = lax.broadcasted_iota(jnp.int32, half_score.shape, 0) + start
                if start < PIX:
                    hit = position == columns[0]
                elif start < PIX + PIX // 4:
                    hit = position == columns[1]
                else:
                    hit = (position == columns[2]) | (position == columns[3])
                value = jnp.tanh(half_score - 1.0) + jnp.where(hit, -1.0, 1.0)
                dscore[start : start + size, :] = value.astype(jnp.bfloat16)
            level_grad[...] = matmul(dscore[...], features, NN)
            grad_rows[...] += matmul(dscore[...], pyramid[...], TN)
            coarse = level_grad[PIX:CELLS, :].astype(jnp.bfloat16)
            gradient = level_grad[0:PIX, :] + matmul(unpool[...], coarse, NN)
            gradient = gradient * 2.0**-5
            convolve_back(gradient, weight_back, moved, total_two, first)

        return carry

    lax.fori_loop(0, SLOTS, slot, 0)

    def rows(total, row, size=1):
        return total[pl.ds(pl.multiple_of(row * TC, TC), size * TC), :].reshape(size, TC, CIN)

    def out(n, block, target):
        return pltpu.make_async_copy(block, target, sems.at[n])

    behind[...] = rows(total_two, at(-2 * side), TR)
    out(0, behind, behind_hbm).start()
    far_out[...] = rows(total_two, edge(-side)).astype(jnp.bfloat16)
    out(1, far_out, far_hbm).start()
    ahead[...] = rows(total_two, at(2 * side), TR)
    out(2, ahead, ahead_hbm).start()
    sum_two[...] = rows(total_two, at(0), TR)
    out(3, sum_two, sum_two_hbm).start()
    to_sibling[0:TR] = rows(total_two, at(side), TR).astype(jnp.bfloat16)
    to_sibling[TR : 2 * TR] = rows(total_two, at(-side), TR).astype(jnp.bfloat16)
    to_sibling[2 * TR : 2 * TR + 1] = rows(total_two, edge(side)).astype(jnp.bfloat16)
    convolve_back(grad_rows[...], weight_back, moved, total_one, 0)
    facing = jnp.where(side > 0, TR + 1, 0)
    outer = jnp.where(side > 0, 0, TR + 1)
    to_sibling[2 * TR + 1 : 2 * TR + 2] = rows(total_one, facing).astype(jnp.bfloat16)
    to_sibling[2 * TR + 2 : 2 * TR + 3] = rows(total_one, outer).astype(jnp.bfloat16)
    out(4, to_sibling, to_sibling_hbm).start()
    sum_one[...] = rows(total_one, 1, TR)
    out(5, sum_one, sum_one_hbm).start()
    out(0, behind, behind_hbm).wait()
    out(1, far_out, far_hbm).wait()
    out(2, ahead, ahead_hbm).wait()
    out(3, sum_two, sum_two_hbm).wait()
    out(4, to_sibling, to_sibling_hbm).wait()
    out(5, sum_one, sum_one_hbm).wait()


def call(kernel, outs, scratch, args, name, scalars, space):
    smem = pl.BlockSpec(memory_space=pltpu.SMEM)
    vmem = pl.BlockSpec(memory_space=pltpu.VMEM)
    return pl.pallas_call(
        kernel,
        in_specs=[smem] * scalars + [vmem] * (len(args) - scalars),
        out_specs=[pl.BlockSpec(memory_space=space)] * len(outs),
        out_shape=[jax.ShapeDtypeStruct(*out) for out in outs],
        scratch_shapes=scratch,
        compiler_params=pltpu.CompilerParams(vmem_limit_bytes=LIMIT << 20),
        name=name,
    )(*args)


def label_rows(targets):
    value = targets.reshape(PIX)
    inside = value % PIX
    row, column = inside // TC, inside % TC
    rows = []
    offset = 0
    for level in range(LEVELS):
        rows.append(offset + (row >> level) * (TC >> level) + (column >> level))
        offset += PIX >> (2 * level)
    rows.append(value // PIX)
    rows += [rows[-1]] * 3
    return jnp.stack(rows).astype(jnp.int32)


def on_device(frame_one, frame_two, conv_weight, partners, counts, targets):
    route = routes(lax.axis_size("tile"))
    index = lax.axis_index("tile")
    side = 1 - 2 * (index % 2)
    f32, bf16 = jnp.float32, jnp.bfloat16

    def send(block, name):
        return lax.ppermute(block, "tile", route[name])

    def row_of(frame, first):
        return lax.dynamic_slice_in_dim(frame, jnp.where(first, 0, TR - 1), 1, 0)

    plan = jnp.concatenate(
        [partners[0] - index, counts, side[None], jnp.zeros((2,), jnp.int32)]
    ).astype(jnp.int32)
    labels = label_rows(targets)
    weight = conv_weight.reshape(9 * CIN, CH)
    near = send(frame_two, "behind")
    direct = send(frame_two, "ahead")
    tables = call(
        tables_kernel,
        [((PAD, PIX), bf16), ((PIX, PAD), bf16)],
        [],
        [],
        "tables",
        0,
        pltpu.VMEM,
    )
    far = send(row_of(frame_two, side > 0), "far")
    cross = send(row_of(frame_one, side > 0), "cross")
    inward = row_of(frame_one, side < 0)
    inward, far, cross, tables, labels, plan = lax.optimization_barrier(
        (inward, far, cross, tables, labels, plan)
    )
    payload = jnp.concatenate([frame_two, near, inward, row_of(direct, side < 0)])
    from_sibling = send(payload, "swap")

    tile = (TR, TC, CIN)
    pack = (2 * TR + 3, TC, CIN)
    outs = [
        (pack, bf16),
        (tile, f32),
        (tile, f32),
        ((1, TC, CIN), bf16),
        (tile, f32),
        (tile, f32),
    ]
    scratch = [
        ((3 * CIN, 3 * CH), bf16),
        ((WIN, TC, CIN), bf16),
        ((WIN * TC, 3 * CIN), bf16),
        ((TR + 2, TC, CIN), bf16),
        (((TR + 2) * TC, 3 * CIN), bf16),
        ((PIX, CH), bf16),
        ((CELLS, CH), bf16),
        ((CELLS, PIX), bf16),
        ((CELLS, CH), f32),
        ((PIX, CH), f32),
        ((PIX, 3 * CH), bf16),
        ((WIN * TC, CIN), f32),
        (((TR + 2) * TC, CIN), f32),
    ]
    to_sibling, ahead, behind, far_out, sum_one, sum_two = call(
        work_kernel,
        outs,
        [pltpu.VMEM(*out) for out in outs]
        + [pltpu.SemaphoreType.DMA((len(outs),))]
        + [pltpu.VMEM(*item) for item in scratch],
        [plan, frame_one, frame_two, near, direct, far, cross]
        + [from_sibling, weight, *tables, labels],
        "work",
        1,
        pltpu.HBM,
    )
    row = lax.broadcasted_iota(jnp.int32, (TR, 1, 1), 0)
    facing = row == jnp.where(side > 0, TR - 1, 0)
    outer = row == jnp.where(side > 0, 0, TR - 1)
    back_sibling = send(to_sibling, "swap")
    ahead_in = (ahead + back_sibling[TR : 2 * TR].astype(f32)).astype(bf16)
    edge = jnp.where(facing, back_sibling[2 * TR : 2 * TR + 1].astype(f32), 0.0)
    behind_in = (behind + edge).astype(bf16)
    back_ahead = send(jnp.concatenate([ahead_in, back_sibling[2 * TR + 2 :]]), "ahead")
    back_behind = send(behind_in, "behind")
    back_far = send(far_out, "far")

    def place(where, block):
        return jnp.where(where, block.astype(f32), 0.0)

    grad_one = sum_one + place(facing, back_sibling[2 * TR + 1 : 2 * TR + 2])
    grad_one = grad_one + place(outer, back_ahead[TR:])
    grad_two = sum_two + back_sibling[:TR].astype(f32) + back_ahead[:TR].astype(f32)
    grad_two = grad_two + back_behind.astype(f32)
    grad_two = grad_two + place(outer, back_far)
    return grad_one.astype(bf16), grad_two.astype(bf16)


def solution(mesh):
    return jax.shard_map(
        on_device,
        mesh=mesh,
        in_specs=(
            P(("groups", "tile"), None, None),
            P(("groups", "tile"), None, None),
            P(),
            P(("groups", "tile"), None),
            P(("groups", "tile")),
            P(("groups", "tile"), None),
        ),
        out_specs=(P(("groups", "tile"), None, None), P(("groups", "tile"), None, None)),
        check_vma=False,
    )
```

```python
import functools

import jax
import jax.numpy as jnp
import numpy as np
from jax import lax
from jax.experimental import pallas as pl
from jax.experimental.pallas import tpu as pltpu
from jax.sharding import PartitionSpec as P

LEVELS = 4
RADIUS = 2
SLOTS = 4
TR = 8
TC = 128
PIX = TR * TC
CIN = 128
CH = 256
POOLED = PIX // 4 + PIX // 16 + PIX // 64
PAD = 384
CELLS = PIX + PAD
LIMIT = 48
WIN = 2 * RADIUS * TR + TR + 2

NN = (((1,), (0,)), ((), ()))
NT = (((1,), (1,)), ((), ()))
TN = (((0,), (0,)), ((), ()))


def matmul(a, b, dims):
    return lax.dot_general(a, b, dims, preferred_element_type=jnp.float32)


def routes(count):
    side = [1 - 2 * (i % 2) for i in range(count)]

    def keep(pairs):
        return [(a, b) for a, b in pairs if 0 <= b < count]

    return dict(
        swap=[(i, i + side[i]) for i in range(count)],
        ahead=keep((i, i + 2 * side[i]) for i in range(count)),
        behind=keep((i, i - 2 * side[i]) for i in range(count)),
        far=keep((i, i - 3 * side[i]) for i in range(count)),
    )


def shifted(block):
    n = block.shape[0]
    column = lax.broadcasted_iota(jnp.int32, block.shape, 0)
    down = jnp.where(column == 0, 0.0, pltpu.roll(block, 1, 0))
    up = jnp.where(column == n - 1, 0.0, pltpu.roll(block, n - 1, 0))
    return down, up


def spread_columns(source, row, target, at):
    middle = source[row]
    down, up = shifted(middle.astype(jnp.float32))
    where = pl.ds(pl.multiple_of(at * TC, TC), TC)
    target[where, 0:CIN] = down.astype(jnp.bfloat16)
    target[where, CIN : 2 * CIN] = middle
    target[where, 2 * CIN : 3 * CIN] = up.astype(jnp.bfloat16)


def convolve(spread, at, weight):
    parts = [
        spread[pl.ds(pl.multiple_of((at + a) * TC, TC), PIX), :] for a in range(3)
    ]
    total = matmul(jnp.concatenate(parts, 1), weight[...], NN)
    return total.astype(jnp.bfloat16)


def convolve_back(gradient, weight_back, moved, total, at):
    for r in range(TR):
        block = gradient[r * TC : (r + 1) * TC, :]
        down, up = shifted(block)
        rows = slice(r * TC, (r + 1) * TC)
        moved[rows, 0:CH] = up.astype(jnp.bfloat16)
        moved[rows, CH : 2 * CH] = block.astype(jnp.bfloat16)
        moved[rows, 2 * CH : 3 * CH] = down.astype(jnp.bfloat16)
    parts = matmul(moved[...], weight_back[...], NT)
    for a in range(3):
        where = pl.ds(pl.multiple_of((at + a) * TC, TC), PIX)
        total[where, :] += parts[:, a * CIN : (a + 1) * CIN]


def pool_matrix(shape, cell_axis, values):
    cell = lax.broadcasted_iota(jnp.int32, shape, cell_axis)
    pixel = lax.broadcasted_iota(jnp.int32, shape, 1 - cell_axis)
    row, column = pixel // TC, pixel % TC
    offset = 0
    result = jnp.zeros(shape, jnp.float32)
    for level in range(1, LEVELS):
        own = offset + (row >> level) * (TC >> level) + (column >> level)
        result = jnp.where(cell == own, values[level], result)
        offset += PIX >> (2 * level)
    return result.astype(jnp.bfloat16)


def per_level(values, fill):
    cell = lax.broadcasted_iota(jnp.int32, (PAD, 1), 0)
    result = jnp.full((PAD, 1), fill, jnp.float32)
    offset = 0
    for level in range(1, LEVELS):
        result = jnp.where(cell >= offset, values[level], result)
        offset += PIX >> (2 * level)
    return jnp.where(cell >= offset, fill, result)


def tile_side():
    return 1 - 2 * lax.rem(lax.axis_index("tile"), 2)


def tables_kernel(pool, unpool):
    pool[...] = pool_matrix((PAD, PIX), 0, [1.0] * LEVELS)
    unpool[...] = pool_matrix((PIX, PAD), 1, [2.0**-level for level in range(LEVELS)])


def rows_kernel(one, two, near, far, inward, sems):
    side = tile_side()
    facing = jnp.where(side > 0, TR - 1, 0)
    outer = jnp.where(side > 0, 0, TR - 1)
    copies = [
        pltpu.make_async_copy(two, near.at[pl.ds(0, TR)], sems.at[0]),
        pltpu.make_async_copy(one.at[pl.ds(outer, 1)], near.at[pl.ds(TR, 1)], sems.at[1]),
        pltpu.make_async_copy(two.at[pl.ds(outer, 1)], far, sems.at[2]),
        pltpu.make_async_copy(one.at[pl.ds(facing, 1)], inward, sems.at[3]),
    ]
    for copy in copies:
        copy.start()
    for copy in copies:
        copy.wait()


def write_labels(targets, labels):
    value = targets[...]
    inside = value % PIX
    row, column = inside // TC, inside % TC
    offset = 0
    for level in range(LEVELS):
        cells = offset + (row >> level) * (TC >> level) + (column >> level)
        for r in range(TR):
            labels[level : level + 1, r * TC : (r + 1) * TC] = cells[r : r + 1, :]
        offset += PIX >> (2 * level)
    slots = value // PIX
    for r in range(TR):
        labels[LEVELS : LEVELS + 1, r * TC : (r + 1) * TC] = slots[r : r + 1, :]


def work_kernel(
    partners,
    counts,
    own_one,
    own_two,
    near,
    direct,
    far,
    from_sibling,
    weight,
    pool,
    unpool,
    targets,
    to_sibling_hbm,
    ahead_hbm,
    behind_hbm,
    far_hbm,
    sum_one_hbm,
    sum_two_hbm,
    to_sibling,
    ahead,
    behind,
    far_out,
    sum_one,
    sum_two,
    sems,
    weight_back,
    labels,
    window,
    spread_two,
    window_one,
    spread_one,
    feat_one,
    pyramid,
    dscore,
    level_grad,
    grad_rows,
    moved,
    total_two,
    total_one,
):
    index = lax.axis_index("tile")
    side = tile_side()
    count = counts[0]

    def at(offset):
        return 1 + TR * (offset + RADIUS)

    def edge(sign):
        return jnp.where(sign > 0, WIN - 1, 0)

    for r in range(TR):
        window[at(0) + r] = own_two[r]
        window[at(2 * side) + r] = near[r]
        window[at(-2 * side) + r] = direct[r]
        window[at(side) + r] = from_sibling[r]
        window[at(-side) + r] = from_sibling[TR + r]
        window_one[1 + r] = own_one[r]
    window[edge(side)] = from_sibling[2 * TR + 2]
    window[edge(-side)] = far[0]
    window_one[jnp.where(side > 0, TR + 1, 0)] = from_sibling[2 * TR + 1]
    window_one[jnp.where(side > 0, 0, TR + 1)] = from_sibling[2 * TR]
    write_labels(targets, labels)

    for a in range(3):
        for b in range(3):
            weight_back[a * CIN : (a + 1) * CIN, b * CH : (b + 1) * CH] = weight[
                (3 * a + b) * CIN : (3 * a + b + 1) * CIN, :
            ]

    def spread(r, carry):
        spread_columns(window, r, spread_two, r)
        return carry

    lax.fori_loop(0, WIN, spread, 0)
    for r in range(TR + 2):
        spread_columns(window_one, r, spread_one, r)
    feat_one[...] = convolve(spread_one, 0, weight)
    grad_rows[...] = jnp.zeros_like(grad_rows)
    total_two[...] = jnp.zeros_like(total_two)
    total_one[...] = jnp.zeros_like(total_one)

    def work_slot(k):
        first = TR * (partners[0, k] - index + RADIUS)
        feat_two = convolve(spread_two, first, weight)
        pyramid[0:PIX, :] = feat_two * jnp.bfloat16(2.0**-5)
        means = matmul(pool[...], feat_two, NN) * per_level(
            [4.0**-level for level in range(LEVELS)], 0.0
        )
        scale = per_level([2.0 ** (level - 5) for level in range(LEVELS)], 0.0)
        pyramid[PIX:CELLS, :] = (
            means.astype(jnp.bfloat16).astype(jnp.float32) * scale
        ).astype(jnp.bfloat16)
        features = feat_one[...]
        here = labels[LEVELS : LEVELS + 1, :] == k
        columns = [jnp.where(here, labels[m : m + 1, :], -1) for m in range(LEVELS)]
        for start in range(0, CELLS, 256):
            size = min(256, CELLS - start)
            half_score = matmul(pyramid[start : start + size, :], features, NT)
            position = lax.broadcasted_iota(jnp.int32, half_score.shape, 0) + start
            if start < PIX:
                hit = position == columns[0]
            elif start < PIX + PIX // 4:
                hit = position == columns[1]
            else:
                hit = (position == columns[2]) | (position == columns[3])
            value = jnp.tanh(half_score - 1.0) + jnp.where(hit, -1.0, 1.0)
            dscore[start : start + size, :] = value.astype(jnp.bfloat16)
        level_grad[...] = matmul(dscore[...], features, NN)
        grad_rows[...] += matmul(dscore[...], pyramid[...], TN)
        coarse = level_grad[PIX:CELLS, :].astype(jnp.bfloat16)
        gradient = level_grad[0:PIX, :] + matmul(unpool[...], coarse, NN)
        level_grad[0:PIX, :] = gradient * 2.0**-5
        convolve_back(level_grad, weight_back, moved, total_two, first)

    def slot(k, carry):
        pl.when(k < count)(lambda: work_slot(k))
        return carry

    lax.fori_loop(0, SLOTS, slot, 0)

    def rows(total, row, size=1):
        return total[pl.ds(pl.multiple_of(row * TC, TC), size * TC), :].reshape(size, TC, CIN)

    def out(n, block, target):
        return pltpu.make_async_copy(block, target, sems.at[n])

    behind[...] = rows(total_two, at(-2 * side), TR)
    out(0, behind, behind_hbm).start()
    far_out[...] = rows(total_two, edge(-side)).astype(jnp.bfloat16)
    out(1, far_out, far_hbm).start()
    ahead[...] = rows(total_two, at(2 * side), TR)
    out(2, ahead, ahead_hbm).start()
    sum_two[...] = rows(total_two, at(0), TR)
    out(3, sum_two, sum_two_hbm).start()
    to_sibling[0:TR] = rows(total_two, at(side), TR).astype(jnp.bfloat16)
    to_sibling[TR : 2 * TR] = rows(total_two, at(-side), TR).astype(jnp.bfloat16)
    to_sibling[2 * TR : 2 * TR + 1] = rows(total_two, edge(side)).astype(jnp.bfloat16)
    convolve_back(grad_rows, weight_back, moved, total_one, 0)
    facing = jnp.where(side > 0, TR + 1, 0)
    outer = jnp.where(side > 0, 0, TR + 1)
    to_sibling[2 * TR + 1 : 2 * TR + 2] = rows(total_one, facing).astype(jnp.bfloat16)
    to_sibling[2 * TR + 2 : 2 * TR + 3] = rows(total_one, outer).astype(jnp.bfloat16)
    out(4, to_sibling, to_sibling_hbm).start()
    sum_one[...] = rows(total_one, 1, TR)
    out(5, sum_one, sum_one_hbm).start()
    out(0, behind, behind_hbm).wait()
    out(1, far_out, far_hbm).wait()
    out(2, ahead, ahead_hbm).wait()
    out(3, sum_two, sum_two_hbm).wait()
    out(4, to_sibling, to_sibling_hbm).wait()
    out(5, sum_one, sum_one_hbm).wait()


def call(kernel, outs, scratch, args, name, in_spaces, out_spaces):
    return pl.pallas_call(
        kernel,
        in_specs=[pl.BlockSpec(memory_space=space) for space in in_spaces],
        out_specs=[pl.BlockSpec(memory_space=space) for space in out_spaces],
        out_shape=[jax.ShapeDtypeStruct(*out) for out in outs],
        scratch_shapes=scratch,
        compiler_params=pltpu.CompilerParams(vmem_limit_bytes=LIMIT << 20),
        name=name,
    )(*args)


def on_device(frame_one, frame_two, conv_weight, partners, counts, targets):
    route = routes(lax.axis_size("tile"))
    index = lax.axis_index("tile")
    side = 1 - 2 * (index % 2)
    f32, bf16 = jnp.float32, jnp.bfloat16

    def send(block, name):
        return lax.ppermute(block, "tile", route[name])

    row_block = (1, TC, CIN)
    weight = conv_weight.reshape(9 * CIN, CH)
    direct = send(frame_two, "ahead")
    near_in, far_in, inward = call(
        rows_kernel,
        [((TR + 1, TC, CIN), bf16), (row_block, bf16), (row_block, bf16)],
        [pltpu.SemaphoreType.DMA((4,))],
        [frame_one, frame_two],
        "rows",
        [pltpu.HBM] * 2,
        [pltpu.HBM] * 3,
    )
    near = send(near_in, "behind")
    far = send(far_in, "far")
    pool, unpool = call(
        tables_kernel,
        [((PAD, PIX), bf16), ((PIX, PAD), bf16)],
        [],
        [],
        "tables",
        [],
        [pltpu.VMEM] * 2,
    )
    inward, far, pool, unpool = lax.optimization_barrier((inward, far, pool, unpool))
    facing_row = jnp.where(side > 0, TR - 1, 0)
    direct_row = lax.dynamic_slice_in_dim(direct, facing_row, 1, 0)
    payload = jnp.concatenate([frame_two, near, inward, direct_row])
    from_sibling = send(payload, "swap")

    tile = (TR, TC, CIN)
    pack = (2 * TR + 3, TC, CIN)
    outs = [
        (pack, bf16),
        (tile, f32),
        (tile, f32),
        ((1, TC, CIN), bf16),
        (tile, f32),
        (tile, f32),
    ]
    scratch = [
        ((3 * CIN, 3 * CH), bf16),
        ((8, PIX), jnp.int32),
        ((WIN, TC, CIN), bf16),
        ((WIN * TC, 3 * CIN), bf16),
        ((TR + 2, TC, CIN), bf16),
        (((TR + 2) * TC, 3 * CIN), bf16),
        ((PIX, CH), bf16),
        ((CELLS, CH), bf16),
        ((CELLS, PIX), bf16),
        ((CELLS, CH), f32),
        ((PIX, CH), f32),
        ((PIX, 3 * CH), bf16),
        ((WIN * TC, CIN), f32),
        (((TR + 2) * TC, CIN), f32),
    ]
    to_sibling, ahead, behind, far_out, sum_one, sum_two = call(
        work_kernel,
        outs,
        [pltpu.VMEM(*out) for out in outs]
        + [pltpu.SemaphoreType.DMA((len(outs),))]
        + [pltpu.VMEM(*item) for item in scratch],
        [partners, counts, frame_one, frame_two, near, direct, far]
        + [from_sibling, weight, pool, unpool, targets],
        "work",
        [pltpu.SMEM] * 2 + [pltpu.VMEM] * 10,
        [pltpu.HBM] * len(outs),
    )
    row = lax.broadcasted_iota(jnp.int32, (TR, 1, 1), 0)
    facing = row == jnp.where(side > 0, TR - 1, 0)
    outer = row == jnp.where(side > 0, 0, TR - 1)
    back_sibling = send(to_sibling, "swap")
    ahead_in = (ahead + back_sibling[TR : 2 * TR].astype(f32)).astype(bf16)
    edge = jnp.where(facing, back_sibling[2 * TR : 2 * TR + 1].astype(f32), 0.0)
    behind_in = (behind + edge).astype(bf16)
    back_ahead = send(jnp.concatenate([ahead_in, back_sibling[2 * TR + 2 :]]), "ahead")
    back_behind = send(behind_in, "behind")
    back_far = send(far_out, "far")

    def place(where, block):
        return jnp.where(where, block.astype(f32), 0.0)

    grad_one = sum_one + place(facing, back_sibling[2 * TR + 1 : 2 * TR + 2])
    grad_one = grad_one + place(outer, back_ahead[TR:])
    grad_two = sum_two + back_sibling[:TR].astype(f32) + back_ahead[:TR].astype(f32)
    grad_two = grad_two + back_behind.astype(f32)
    grad_two = grad_two + place(outer, back_far)
    return grad_one.astype(bf16), grad_two.astype(bf16)


def solution(mesh):
    return jax.shard_map(
        on_device,
        mesh=mesh,
        in_specs=(
            P(("groups", "tile"), None, None),
            P(("groups", "tile"), None, None),
            P(),
            P(("groups", "tile"), None),
            P(("groups", "tile")),
            P(("groups", "tile"), None),
        ),
        out_specs=(P(("groups", "tile"), None, None), P(("groups", "tile"), None, None)),
        check_vma=False,
    )
```

```python
import functools

import jax
import jax.numpy as jnp
import numpy as np
from jax import lax
from jax.experimental import pallas as pl
from jax.experimental.pallas import tpu as pltpu
from jax.sharding import PartitionSpec as P

LEVELS = 4
RADIUS = 2
SLOTS = 4
TR = 8
TC = 128
PIX = TR * TC
CIN = 128
CH = 256
POOLED = PIX // 4 + PIX // 16 + PIX // 64
PAD = 384
CELLS = PIX + PAD
CHUNK = 256
LIMIT = 50
WIN = 2 * RADIUS * TR + TR + 2

NN = (((1,), (0,)), ((), ()))
NT = (((1,), (1,)), ((), ()))
TN = (((0,), (0,)), ((), ()))


def matmul(a, b, dims):
    return lax.dot_general(a, b, dims, preferred_element_type=jnp.float32)


def routes(count):
    side = [1 - 2 * (i % 2) for i in range(count)]

    def keep(pairs):
        return [(a, b) for a, b in pairs if 0 <= b < count]

    return dict(
        swap=[(i, i + side[i]) for i in range(count)],
        ahead=keep((i, i + 2 * side[i]) for i in range(count)),
        behind=keep((i, i - 2 * side[i]) for i in range(count)),
        far=keep((i, i - 3 * side[i]) for i in range(count)),
        cross=keep((i, i - side[i]) for i in range(count)),
    )


def shifted(block):
    n = block.shape[0]
    column = lax.broadcasted_iota(jnp.int32, block.shape, 0)
    down = jnp.where(column == 0, 0.0, pltpu.roll(block, 1, 0))
    up = jnp.where(column == n - 1, 0.0, pltpu.roll(block, n - 1, 0))
    return down, up


def spread_columns(source, row, target, at):
    middle = source[row]
    down, up = shifted(middle.astype(jnp.float32))
    where = pl.ds(pl.multiple_of(at * TC, TC), TC)
    target[where, 0:CIN] = down.astype(jnp.bfloat16)
    target[where, CIN : 2 * CIN] = middle
    target[where, 2 * CIN : 3 * CIN] = up.astype(jnp.bfloat16)


def convolve(spread, at, weight):
    parts = [
        spread[pl.ds(pl.multiple_of((at + a) * TC, TC), PIX), :] for a in range(3)
    ]
    total = matmul(jnp.concatenate(parts, 1), weight[...], NN)
    return total.astype(jnp.bfloat16)


def spread_back(gradient, moved):
    for r in range(TR):
        rows = slice(r * TC, (r + 1) * TC)
        block = gradient[rows, :]
        down, up = shifted(block)
        moved[rows, 0:CH] = up.astype(jnp.bfloat16)
        moved[rows, CH : 2 * CH] = block.astype(jnp.bfloat16)
        moved[rows, 2 * CH : 3 * CH] = down.astype(jnp.bfloat16)


def convolve_back(moved, weight_back, total, at):
    parts = matmul(moved[...], weight_back[...], NT)
    for a in range(3):
        where = pl.ds(pl.multiple_of((at + a) * TC, TC), PIX)
        total[where, :] += parts[:, a * CIN : (a + 1) * CIN]


def pool_matrix(shape, cell_axis, values):
    cell = lax.broadcasted_iota(jnp.int32, shape, cell_axis)
    pixel = lax.broadcasted_iota(jnp.int32, shape, 1 - cell_axis)
    row, column = pixel // TC, pixel % TC
    offset = 0
    result = jnp.zeros(shape, jnp.float32)
    for level in range(1, LEVELS):
        own = offset + (row >> level) * (TC >> level) + (column >> level)
        result = jnp.where(cell == own, values[level], result)
        offset += PIX >> (2 * level)
    return result.astype(jnp.bfloat16)


def per_level(values, fill):
    cell = lax.broadcasted_iota(jnp.int32, (PAD, 1), 0)
    result = jnp.full((PAD, 1), fill, jnp.float32)
    offset = 0
    for level in range(1, LEVELS):
        result = jnp.where(cell >= offset, values[level], result)
        offset += PIX >> (2 * level)
    return jnp.where(cell >= offset, fill, result)


def tile_side():
    return 1 - 2 * lax.rem(lax.axis_index("tile"), 2)


def tables_kernel(pool, unpool):
    pool[...] = pool_matrix((PAD, PIX), 0, [1.0] * LEVELS)
    unpool[...] = pool_matrix((PIX, PAD), 1, [2.0**-level for level in range(LEVELS)])


def rows_kernel(one, two, cross, far, inward, sems):
    side = tile_side()
    facing = jnp.where(side > 0, TR - 1, 0)
    outer = jnp.where(side > 0, 0, TR - 1)
    copies = [
        pltpu.make_async_copy(one.at[pl.ds(outer, 1)], cross, sems.at[0]),
        pltpu.make_async_copy(two.at[pl.ds(outer, 1)], far, sems.at[1]),
        pltpu.make_async_copy(one.at[pl.ds(facing, 1)], inward, sems.at[2]),
    ]
    for copy in copies:
        copy.start()
    for copy in copies:
        copy.wait()


def write_labels(targets, labels):
    value = targets[...]
    inside = value % PIX
    row, column = inside // TC, inside % TC
    offset = 0
    for level in range(LEVELS):
        cells = offset + (row >> level) * (TC >> level) + (column >> level)
        for r in range(TR):
            labels[level : level + 1, r * TC : (r + 1) * TC] = cells[r : r + 1, :]
        offset += PIX >> (2 * level)
    slots = value // PIX
    for r in range(TR):
        labels[LEVELS : LEVELS + 1, r * TC : (r + 1) * TC] = slots[r : r + 1, :]


def work_kernel(
    partners,
    counts,
    own_one,
    own_two,
    near,
    direct,
    far,
    cross,
    from_sibling,
    weight,
    pool,
    unpool,
    targets,
    to_sibling_hbm,
    ahead_hbm,
    behind_hbm,
    far_hbm,
    sum_one_hbm,
    sum_two_hbm,
    to_sibling,
    ahead,
    behind,
    far_out,
    sum_one,
    sum_two,
    sems,
    weight_back,
    labels,
    window,
    spread_two,
    window_one,
    spread_one,
    feat_one,
    feat_two,
    pyramid,
    dscore,
    level_grad,
    grad_rows,
    moved,
    total_two,
    total_one,
):
    index = lax.axis_index("tile")
    side = tile_side()
    count = counts[0]

    def at(offset):
        return 1 + TR * (offset + RADIUS)

    def edge(sign):
        return jnp.where(sign > 0, WIN - 1, 0)

    for r in range(TR):
        window[at(0) + r] = own_two[r]
        window[at(2 * side) + r] = near[r]
        window[at(-2 * side) + r] = direct[r]
        window[at(side) + r] = from_sibling[r]
        window[at(-side) + r] = from_sibling[TR + r]
        window_one[1 + r] = own_one[r]
    window[edge(side)] = from_sibling[2 * TR + 1]
    window[edge(-side)] = far[0]
    window_one[jnp.where(side > 0, TR + 1, 0)] = from_sibling[2 * TR]
    window_one[jnp.where(side > 0, 0, TR + 1)] = cross[0]
    write_labels(targets, labels)

    for a in range(3):
        for b in range(3):
            weight_back[a * CIN : (a + 1) * CIN, b * CH : (b + 1) * CH] = weight[
                (3 * a + b) * CIN : (3 * a + b + 1) * CIN, :
            ]

    def spread(r, carry):
        spread_columns(window, r, spread_two, r)
        return carry

    lax.fori_loop(0, WIN, spread, 0)
    for r in range(TR + 2):
        spread_columns(window_one, r, spread_one, r)
    feat_one[...] = convolve(spread_one, 0, weight)
    grad_rows[...] = jnp.zeros_like(grad_rows)
    total_two[...] = jnp.zeros_like(total_two)
    total_one[...] = jnp.zeros_like(total_one)

    def first_row(k):
        return TR * (partners[0, k] - index + RADIUS)

    feat_two[...] = convolve(spread_two, first_row(0), weight)

    def work_slot(k):
        features = feat_one[...]
        here = labels[LEVELS : LEVELS + 1, :] == k
        columns = [jnp.where(here, labels[m : m + 1, :], -1) for m in range(LEVELS)]

        def score(start, size, hits):
            half_score = matmul(pyramid[start : start + size, :], features, NT)
            position = lax.broadcasted_iota(jnp.int32, half_score.shape, 0) + start
            hit = position == hits[0]
            for more in hits[1:]:
                hit = hit | (position == more)
            value = jnp.tanh(half_score - 1.0) + jnp.where(hit, -1.0, 1.0)
            dscore[start : start + size, :] = value.astype(jnp.bfloat16)

        pyramid[0:PIX, :] = feat_two[...] * jnp.bfloat16(2.0**-5)
        score(0, CHUNK, columns[:1])
        means = matmul(pool[...], feat_two[...], NN) * per_level(
            [4.0**-level for level in range(LEVELS)], 0.0
        )
        scale = per_level([2.0 ** (level - 5) for level in range(LEVELS)], 0.0)
        pyramid[PIX:CELLS, :] = (
            means.astype(jnp.bfloat16).astype(jnp.float32) * scale
        ).astype(jnp.bfloat16)
        for start in range(CHUNK, PIX, CHUNK):
            score(start, CHUNK, columns[:1])
        score(PIX, PIX // 4, columns[1:2])
        score(PIX + PIX // 4, PAD - PIX // 4, columns[2:])
        level_grad[PIX:CELLS, :] = matmul(dscore[PIX:CELLS, :], features, NN)
        level_grad[0:PIX, :] = matmul(dscore[0:PIX, :], features, NN)
        coarse = level_grad[PIX:CELLS, :].astype(jnp.bfloat16)
        gradient = level_grad[0:PIX, :] + matmul(unpool[...], coarse, NN)
        level_grad[0:PIX, :] = gradient * 2.0**-5
        spread_back(level_grad, moved)
        feat_two[...] = convolve(spread_two, first_row(jnp.minimum(k + 1, SLOTS - 1)), weight)
        grad_rows[...] += matmul(dscore[...], pyramid[...], TN)
        convolve_back(moved, weight_back, total_two, first_row(k))

    def slot(k, carry):
        pl.when(k < count)(lambda: work_slot(k))
        return carry

    lax.fori_loop(0, SLOTS, slot, 0)

    def rows(total, row, size=1):
        return total[pl.ds(pl.multiple_of(row * TC, TC), size * TC), :].reshape(size, TC, CIN)

    def out(n, block, target):
        return pltpu.make_async_copy(block, target, sems.at[n])

    behind[...] = rows(total_two, at(-2 * side), TR)
    out(0, behind, behind_hbm).start()
    far_out[...] = rows(total_two, edge(-side)).astype(jnp.bfloat16)
    out(1, far_out, far_hbm).start()
    ahead[...] = rows(total_two, at(2 * side), TR)
    out(2, ahead, ahead_hbm).start()
    sum_two[...] = rows(total_two, at(0), TR)
    out(3, sum_two, sum_two_hbm).start()
    to_sibling[0:TR] = rows(total_two, at(side), TR).astype(jnp.bfloat16)
    to_sibling[TR : 2 * TR] = rows(total_two, at(-side), TR).astype(jnp.bfloat16)
    to_sibling[2 * TR : 2 * TR + 1] = rows(total_two, edge(side)).astype(jnp.bfloat16)
    spread_back(grad_rows, moved)
    convolve_back(moved, weight_back, total_one, 0)
    facing = jnp.where(side > 0, TR + 1, 0)
    outer = jnp.where(side > 0, 0, TR + 1)
    to_sibling[2 * TR + 1 : 2 * TR + 2] = rows(total_one, facing).astype(jnp.bfloat16)
    to_sibling[2 * TR + 2 : 2 * TR + 3] = rows(total_one, outer).astype(jnp.bfloat16)
    out(4, to_sibling, to_sibling_hbm).start()
    sum_one[...] = rows(total_one, 1, TR)
    out(5, sum_one, sum_one_hbm).start()
    out(0, behind, behind_hbm).wait()
    out(1, far_out, far_hbm).wait()
    out(2, ahead, ahead_hbm).wait()
    out(3, sum_two, sum_two_hbm).wait()
    out(4, to_sibling, to_sibling_hbm).wait()
    out(5, sum_one, sum_one_hbm).wait()


def call(kernel, outs, scratch, args, name, in_spaces, out_spaces):
    return pl.pallas_call(
        kernel,
        in_specs=[pl.BlockSpec(memory_space=space) for space in in_spaces],
        out_specs=[pl.BlockSpec(memory_space=space) for space in out_spaces],
        out_shape=[jax.ShapeDtypeStruct(*out) for out in outs],
        scratch_shapes=scratch,
        compiler_params=pltpu.CompilerParams(vmem_limit_bytes=LIMIT << 20),
        name=name,
    )(*args)


def on_device(frame_one, frame_two, conv_weight, partners, counts, targets):
    route = routes(lax.axis_size("tile"))
    index = lax.axis_index("tile")
    side = 1 - 2 * (index % 2)
    f32, bf16 = jnp.float32, jnp.bfloat16

    def send(block, name):
        return lax.ppermute(block, "tile", route[name])

    row_block = (1, TC, CIN)
    weight = conv_weight.reshape(9 * CIN, CH)
    direct = send(frame_two, "ahead")
    near = send(frame_two, "behind")
    cross_in, far_in, inward = call(
        rows_kernel,
        [(row_block, bf16)] * 3,
        [pltpu.SemaphoreType.DMA((3,))],
        [frame_one, frame_two],
        "rows",
        [pltpu.HBM] * 2,
        [pltpu.HBM] * 3,
    )
    far = send(far_in, "far")
    cross = send(cross_in, "cross")
    pool, unpool = call(
        tables_kernel,
        [((PAD, PIX), bf16), ((PIX, PAD), bf16)],
        [],
        [],
        "tables",
        [],
        [pltpu.VMEM] * 2,
    )
    inward, far, cross, pool, unpool = lax.optimization_barrier(
        (inward, far, cross, pool, unpool)
    )
    facing_row = jnp.where(side > 0, TR - 1, 0)
    direct_row = lax.dynamic_slice_in_dim(direct, facing_row, 1, 0)
    payload = jnp.concatenate([frame_two, near, inward, direct_row])
    from_sibling = send(payload, "swap")

    tile = (TR, TC, CIN)
    pack = (2 * TR + 3, TC, CIN)
    outs = [
        (pack, bf16),
        (tile, f32),
        (tile, f32),
        ((1, TC, CIN), bf16),
        (tile, f32),
        (tile, f32),
    ]
    scratch = [
        ((3 * CIN, 3 * CH), bf16),
        ((8, PIX), jnp.int32),
        ((WIN, TC, CIN), bf16),
        ((WIN * TC, 3 * CIN), bf16),
        ((TR + 2, TC, CIN), bf16),
        (((TR + 2) * TC, 3 * CIN), bf16),
        ((PIX, CH), bf16),
        ((PIX, CH), bf16),
        ((CELLS, CH), bf16),
        ((CELLS, PIX), bf16),
        ((CELLS, CH), f32),
        ((PIX, CH), f32),
        ((PIX, 3 * CH), bf16),
        ((WIN * TC, CIN), f32),
        (((TR + 2) * TC, CIN), f32),
    ]
    to_sibling, ahead, behind, far_out, sum_one, sum_two = call(
        work_kernel,
        outs,
        [pltpu.VMEM(*out) for out in outs]
        + [pltpu.SemaphoreType.DMA((len(outs),))]
        + [pltpu.VMEM(*item) for item in scratch],
        [partners, counts, frame_one, frame_two, near, direct, far, cross]
        + [from_sibling, weight, pool, unpool, targets],
        "work",
        [pltpu.SMEM] * 2 + [pltpu.VMEM] * 11,
        [pltpu.HBM] * len(outs),
    )
    row = lax.broadcasted_iota(jnp.int32, (TR, 1, 1), 0)
    facing = row == jnp.where(side > 0, TR - 1, 0)
    outer = row == jnp.where(side > 0, 0, TR - 1)
    back_sibling = send(to_sibling, "swap")
    ahead_in = (ahead + back_sibling[TR : 2 * TR].astype(f32)).astype(bf16)
    edge = jnp.where(facing, back_sibling[2 * TR : 2 * TR + 1].astype(f32), 0.0)
    behind_in = (behind + edge).astype(bf16)
    back_ahead = send(jnp.concatenate([ahead_in, back_sibling[2 * TR + 2 :]]), "ahead")
    back_behind = send(behind_in, "behind")
    back_far = send(far_out, "far")

    def place(where, block):
        return jnp.where(where, block.astype(f32), 0.0)

    grad_one = sum_one + place(facing, back_sibling[2 * TR + 1 : 2 * TR + 2])
    grad_one = grad_one + place(outer, back_ahead[TR:])
    grad_two = sum_two + back_sibling[:TR].astype(f32) + back_ahead[:TR].astype(f32)
    grad_two = grad_two + back_behind.astype(f32)
    grad_two = grad_two + place(outer, back_far)
    return grad_one.astype(bf16), grad_two.astype(bf16)


def solution(mesh):
    return jax.shard_map(
        on_device,
        mesh=mesh,
        in_specs=(
            P(("groups", "tile"), None, None),
            P(("groups", "tile"), None, None),
            P(),
            P(("groups", "tile"), None),
            P(("groups", "tile")),
            P(("groups", "tile"), None),
        ),
        out_specs=(P(("groups", "tile"), None, None), P(("groups", "tile"), None, None)),
        check_vma=False,
    )
```

```python
import functools

import jax
import jax.numpy as jnp
import numpy as np
from jax import lax
from jax.experimental import pallas as pl
from jax.experimental.pallas import tpu as pltpu
from jax.sharding import PartitionSpec as P

LEVELS = 4
RADIUS = 2
SLOTS = 4
TR = 8
TC = 128
PIX = TR * TC
CIN = 128
CH = 256
POOLED = PIX // 4 + PIX // 16 + PIX // 64
PAD = 384
CELLS = PIX + PAD
CHUNK = 256
LIMIT = 49
WIN = 2 * RADIUS * TR + TR + 2

NN = (((1,), (0,)), ((), ()))
NT = (((1,), (1,)), ((), ()))
TN = (((0,), (0,)), ((), ()))


def matmul(a, b, dims):
    return lax.dot_general(a, b, dims, preferred_element_type=jnp.float32)


def routes(count):
    side = [1 - 2 * (i % 2) for i in range(count)]

    def keep(pairs):
        return [(a, b) for a, b in pairs if 0 <= b < count]

    return dict(
        swap=[(i, i + side[i]) for i in range(count)],
        ahead=keep((i, i + 2 * side[i]) for i in range(count)),
        behind=keep((i, i - 2 * side[i]) for i in range(count)),
        far=keep((i, i - 3 * side[i]) for i in range(count)),
        cross=keep((i, i - side[i]) for i in range(count)),
    )


def shifted(block):
    n = block.shape[0]
    column = lax.broadcasted_iota(jnp.int32, block.shape, 0)
    down = jnp.where(column == 0, 0.0, pltpu.roll(block, 1, 0))
    up = jnp.where(column == n - 1, 0.0, pltpu.roll(block, n - 1, 0))
    return down, up


def spread_columns(source, row, target, at):
    middle = source[row]
    down, up = shifted(middle.astype(jnp.float32))
    where = pl.ds(pl.multiple_of(at * TC, TC), TC)
    target[where, 0:CIN] = down.astype(jnp.bfloat16)
    target[where, CIN : 2 * CIN] = middle
    target[where, 2 * CIN : 3 * CIN] = up.astype(jnp.bfloat16)


def convolve(spread, at, weight):
    parts = [
        spread[pl.ds(pl.multiple_of((at + a) * TC, TC), PIX), :] for a in range(3)
    ]
    total = matmul(jnp.concatenate(parts, 1), weight[...], NN)
    return total.astype(jnp.bfloat16)


def spread_back(gradient, moved):
    for r in range(TR):
        rows = slice(r * TC, (r + 1) * TC)
        block = gradient[rows, :]
        down, up = shifted(block)
        moved[rows, 0:CH] = up.astype(jnp.bfloat16)
        moved[rows, CH : 2 * CH] = block.astype(jnp.bfloat16)
        moved[rows, 2 * CH : 3 * CH] = down.astype(jnp.bfloat16)


def convolve_back(moved, weight_back, total, at):
    parts = matmul(moved[...], weight_back[...], NT)
    for a in range(3):
        where = pl.ds(pl.multiple_of((at + a) * TC, TC), PIX)
        total[where, :] += parts[:, a * CIN : (a + 1) * CIN]


def pool_matrix(shape, cell_axis, values):
    cell = lax.broadcasted_iota(jnp.int32, shape, cell_axis)
    pixel = lax.broadcasted_iota(jnp.int32, shape, 1 - cell_axis)
    row, column = pixel // TC, pixel % TC
    offset = 0
    result = jnp.zeros(shape, jnp.float32)
    for level in range(1, LEVELS):
        own = offset + (row >> level) * (TC >> level) + (column >> level)
        result = jnp.where(cell == own, values[level], result)
        offset += PIX >> (2 * level)
    return result.astype(jnp.bfloat16)


def per_level(values, fill):
    cell = lax.broadcasted_iota(jnp.int32, (PAD, 1), 0)
    result = jnp.full((PAD, 1), fill, jnp.float32)
    offset = 0
    for level in range(1, LEVELS):
        result = jnp.where(cell >= offset, values[level], result)
        offset += PIX >> (2 * level)
    return jnp.where(cell >= offset, fill, result)


def tile_side():
    return 1 - 2 * lax.rem(lax.axis_index("tile"), 2)


def tables_kernel(pool, unpool):
    pool[...] = pool_matrix((PAD, PIX), 0, [1.0] * LEVELS)
    unpool[...] = pool_matrix((PIX, PAD), 1, [2.0**-level for level in range(LEVELS)])


def rows_kernel(one, two, cross, far, inward, sems):
    side = tile_side()
    facing = jnp.where(side > 0, TR - 1, 0)
    outer = jnp.where(side > 0, 0, TR - 1)
    copies = [
        pltpu.make_async_copy(one.at[pl.ds(outer, 1)], cross, sems.at[0]),
        pltpu.make_async_copy(two.at[pl.ds(outer, 1)], far, sems.at[1]),
        pltpu.make_async_copy(one.at[pl.ds(facing, 1)], inward, sems.at[2]),
    ]
    for copy in copies:
        copy.start()
    for copy in copies:
        copy.wait()


def write_labels(targets, labels):
    value = targets[...]
    inside = value % PIX
    row, column = inside // TC, inside % TC
    offset = 0
    for level in range(LEVELS):
        cells = offset + (row >> level) * (TC >> level) + (column >> level)
        for r in range(TR):
            labels[level : level + 1, r * TC : (r + 1) * TC] = cells[r : r + 1, :]
        offset += PIX >> (2 * level)
    slots = value // PIX
    for r in range(TR):
        labels[LEVELS : LEVELS + 1, r * TC : (r + 1) * TC] = slots[r : r + 1, :]


def work_kernel(
    partners,
    counts,
    own_one,
    own_two,
    near,
    direct,
    far,
    cross,
    from_sibling,
    weight,
    pool,
    unpool,
    targets,
    to_sibling_hbm,
    ahead_hbm,
    behind_hbm,
    far_hbm,
    sum_one_hbm,
    sum_two_hbm,
    to_sibling,
    ahead,
    behind,
    far_out,
    sum_one,
    sum_two,
    sems,
    weight_back,
    labels,
    window,
    spread_two,
    window_one,
    spread_one,
    feat_one,
    feat_two,
    pyramid,
    dscore,
    level_grad,
    grad_rows,
    moved,
    total_two,
    total_one,
):
    index = lax.axis_index("tile")
    side = tile_side()
    count = counts[0]

    def at(offset):
        return 1 + TR * (offset + RADIUS)

    def edge(sign):
        return jnp.where(sign > 0, WIN - 1, 0)

    for r in range(TR):
        window[at(0) + r] = own_two[r]
        window[at(2 * side) + r] = near[r]
        window[at(-2 * side) + r] = direct[r]
        window[at(side) + r] = from_sibling[r]
        window[at(-side) + r] = from_sibling[TR + r]
        window_one[1 + r] = own_one[r]
    window[edge(side)] = from_sibling[2 * TR + 1]
    window[edge(-side)] = far[0]
    window_one[jnp.where(side > 0, TR + 1, 0)] = from_sibling[2 * TR]
    window_one[jnp.where(side > 0, 0, TR + 1)] = cross[0]
    write_labels(targets, labels)

    for a in range(3):
        for b in range(3):
            weight_back[a * CIN : (a + 1) * CIN, b * CH : (b + 1) * CH] = weight[
                (3 * a + b) * CIN : (3 * a + b + 1) * CIN, :
            ]

    def spread(r, carry):
        spread_columns(window, r, spread_two, r)
        return carry

    lax.fori_loop(0, WIN, spread, 0)
    for r in range(TR + 2):
        spread_columns(window_one, r, spread_one, r)
    feat_one[...] = convolve(spread_one, 0, weight)
    grad_rows[...] = jnp.zeros_like(grad_rows)
    total_two[...] = jnp.zeros_like(total_two)
    total_one[...] = jnp.zeros_like(total_one)

    def first_row(k):
        return TR * (partners[0, k] - index + RADIUS)

    feat_two[...] = convolve(spread_two, first_row(0), weight)

    def work_slot(k):
        features = feat_one[...]
        here = labels[LEVELS : LEVELS + 1, :] == k
        columns = [jnp.where(here, labels[m : m + 1, :], -1) for m in range(LEVELS)]

        def score(start, size, hits):
            half_score = matmul(pyramid[start : start + size, :], features, NT)
            position = lax.broadcasted_iota(jnp.int32, half_score.shape, 0) + start
            hit = position == hits[0]
            for more in hits[1:]:
                hit = hit | (position == more)
            value = jnp.tanh(half_score - 1.0) + jnp.where(hit, -1.0, 1.0)
            dscore[start : start + size, :] = value.astype(jnp.bfloat16)

        pyramid[0:PIX, :] = feat_two[...] * jnp.bfloat16(2.0**-5)
        score(0, CHUNK, columns[:1])
        means = matmul(pool[...], feat_two[...], NN) * per_level(
            [4.0**-level for level in range(LEVELS)], 0.0
        )
        scale = per_level([2.0 ** (level - 5) for level in range(LEVELS)], 0.0)
        pyramid[PIX:CELLS, :] = (
            means.astype(jnp.bfloat16).astype(jnp.float32) * scale
        ).astype(jnp.bfloat16)
        for start in range(CHUNK, PIX, CHUNK):
            score(start, CHUNK, columns[:1])
        score(PIX, PIX // 4, columns[1:2])
        score(PIX + PIX // 4, PAD - PIX // 4, columns[2:])
        level_grad[PIX:CELLS, :] = matmul(dscore[PIX:CELLS, :], features, NN)
        level_grad[0:PIX, :] = matmul(dscore[0:PIX, :], features, NN)
        coarse = level_grad[PIX:CELLS, :].astype(jnp.bfloat16)
        gradient = level_grad[0:PIX, :] + matmul(unpool[...], coarse, NN)
        level_grad[0:PIX, :] = gradient * 2.0**-5
        spread_back(level_grad, moved)
        feat_two[...] = convolve(spread_two, first_row(jnp.minimum(k + 1, SLOTS - 1)), weight)
        grad_rows[...] += matmul(dscore[...], pyramid[...], TN)
        convolve_back(moved, weight_back, total_two, first_row(k))

    def slot(k, carry):
        pl.when(k < count)(lambda: work_slot(k))
        return carry

    lax.fori_loop(0, SLOTS, slot, 0)

    def rows(total, row, size=1):
        return total[pl.ds(pl.multiple_of(row * TC, TC), size * TC), :].reshape(size, TC, CIN)

    def out(n, block, target):
        return pltpu.make_async_copy(block, target, sems.at[n])

    behind[...] = rows(total_two, at(-2 * side), TR)
    out(0, behind, behind_hbm).start()
    far_out[...] = rows(total_two, edge(-side)).astype(jnp.bfloat16)
    out(1, far_out, far_hbm).start()
    ahead[...] = rows(total_two, at(2 * side), TR)
    out(2, ahead, ahead_hbm).start()
    sum_two[...] = rows(total_two, at(0), TR)
    out(3, sum_two, sum_two_hbm).start()
    to_sibling[0:TR] = rows(total_two, at(side), TR).astype(jnp.bfloat16)
    to_sibling[TR : 2 * TR] = rows(total_two, at(-side), TR).astype(jnp.bfloat16)
    to_sibling[2 * TR : 2 * TR + 1] = rows(total_two, edge(side)).astype(jnp.bfloat16)
    spread_back(grad_rows, moved)
    convolve_back(moved, weight_back, total_one, 0)
    facing = jnp.where(side > 0, TR + 1, 0)
    outer = jnp.where(side > 0, 0, TR + 1)
    to_sibling[2 * TR + 1 : 2 * TR + 2] = rows(total_one, facing).astype(jnp.bfloat16)
    to_sibling[2 * TR + 2 : 2 * TR + 3] = rows(total_one, outer).astype(jnp.bfloat16)
    out(4, to_sibling, to_sibling_hbm).start()
    sum_one[...] = rows(total_one, 1, TR)
    out(5, sum_one, sum_one_hbm).start()
    out(0, behind, behind_hbm).wait()
    out(1, far_out, far_hbm).wait()
    out(2, ahead, ahead_hbm).wait()
    out(3, sum_two, sum_two_hbm).wait()
    out(4, to_sibling, to_sibling_hbm).wait()
    out(5, sum_one, sum_one_hbm).wait()


def call(kernel, outs, scratch, args, name, in_spaces, out_spaces):
    return pl.pallas_call(
        kernel,
        in_specs=[pl.BlockSpec(memory_space=space) for space in in_spaces],
        out_specs=[pl.BlockSpec(memory_space=space) for space in out_spaces],
        out_shape=[jax.ShapeDtypeStruct(*out) for out in outs],
        scratch_shapes=scratch,
        compiler_params=pltpu.CompilerParams(vmem_limit_bytes=LIMIT << 20),
        name=name,
    )(*args)


def on_device(frame_one, frame_two, conv_weight, partners, counts, targets):
    route = routes(lax.axis_size("tile"))
    index = lax.axis_index("tile")
    side = 1 - 2 * (index % 2)
    f32, bf16 = jnp.float32, jnp.bfloat16

    def send(block, name):
        return lax.ppermute(block, "tile", route[name])

    row_block = (1, TC, CIN)
    weight = conv_weight.reshape(9 * CIN, CH)
    direct = send(frame_two, "ahead")
    near = send(frame_two, "behind")
    cross_in, far_in, inward = call(
        rows_kernel,
        [(row_block, bf16)] * 3,
        [pltpu.SemaphoreType.DMA((3,))],
        [pltpu.with_memory_space_constraint(x, pltpu.HBM) for x in (frame_one, frame_two)],
        "rows",
        [pltpu.HBM] * 2,
        [pltpu.HBM] * 3,
    )
    far = send(far_in, "far")
    cross = send(cross_in, "cross")
    pool, unpool = call(
        tables_kernel,
        [((PAD, PIX), bf16), ((PIX, PAD), bf16)],
        [],
        [],
        "tables",
        [],
        [pltpu.VMEM] * 2,
    )
    inward, far, cross, pool, unpool = lax.optimization_barrier(
        (inward, far, cross, pool, unpool)
    )
    facing_row = jnp.where(side > 0, TR - 1, 0)
    direct_row = lax.dynamic_slice_in_dim(direct, facing_row, 1, 0)
    payload = jnp.concatenate([frame_two, near, inward, direct_row])
    from_sibling = send(payload, "swap")

    tile = (TR, TC, CIN)
    pack = (2 * TR + 3, TC, CIN)
    outs = [
        (pack, bf16),
        (tile, f32),
        (tile, f32),
        ((1, TC, CIN), bf16),
        (tile, f32),
        (tile, f32),
    ]
    scratch = [
        ((3 * CIN, 3 * CH), bf16),
        ((8, PIX), jnp.int32),
        ((WIN, TC, CIN), bf16),
        ((WIN * TC, 3 * CIN), bf16),
        ((TR + 2, TC, CIN), bf16),
        (((TR + 2) * TC, 3 * CIN), bf16),
        ((PIX, CH), bf16),
        ((PIX, CH), bf16),
        ((CELLS, CH), bf16),
        ((CELLS, PIX), bf16),
        ((CELLS, CH), f32),
        ((PIX, CH), f32),
        ((PIX, 3 * CH), bf16),
        ((WIN * TC, CIN), f32),
        (((TR + 2) * TC, CIN), f32),
    ]
    to_sibling, ahead, behind, far_out, sum_one, sum_two = call(
        work_kernel,
        outs,
        [pltpu.VMEM(*out) for out in outs]
        + [pltpu.SemaphoreType.DMA((len(outs),))]
        + [pltpu.VMEM(*item) for item in scratch],
        [partners, counts, frame_one, frame_two, near, direct, far, cross]
        + [from_sibling, weight, pool, unpool, targets],
        "work",
        [pltpu.SMEM] * 2 + [pltpu.VMEM] * 11,
        [pltpu.HBM] * len(outs),
    )
    row = lax.broadcasted_iota(jnp.int32, (TR, 1, 1), 0)
    facing = row == jnp.where(side > 0, TR - 1, 0)
    outer = row == jnp.where(side > 0, 0, TR - 1)
    back_sibling = send(to_sibling, "swap")
    ahead_in = (ahead + back_sibling[TR : 2 * TR].astype(f32)).astype(bf16)
    edge = jnp.where(facing, back_sibling[2 * TR : 2 * TR + 1].astype(f32), 0.0)
    behind_in = (behind + edge).astype(bf16)
    back_ahead = send(jnp.concatenate([ahead_in, back_sibling[2 * TR + 2 :]]), "ahead")
    back_behind = send(behind_in, "behind")
    back_far = send(far_out, "far")

    def place(where, block):
        return jnp.where(where, block.astype(f32), 0.0)

    grad_one = sum_one + place(facing, back_sibling[2 * TR + 1 : 2 * TR + 2])
    grad_one = grad_one + place(outer, back_ahead[TR:])
    grad_two = sum_two + back_sibling[:TR].astype(f32) + back_ahead[:TR].astype(f32)
    grad_two = grad_two + back_behind.astype(f32)
    grad_two = grad_two + place(outer, back_far)
    return grad_one.astype(bf16), grad_two.astype(bf16)


def solution(mesh):
    return jax.shard_map(
        on_device,
        mesh=mesh,
        in_specs=(
            P(("groups", "tile"), None, None),
            P(("groups", "tile"), None, None),
            P(),
            P(("groups", "tile"), None),
            P(("groups", "tile")),
            P(("groups", "tile"), None),
        ),
        out_specs=(P(("groups", "tile"), None, None), P(("groups", "tile"), None, None)),
        check_vma=False,
    )
```

```python
import functools

import jax
import jax.numpy as jnp
import numpy as np
from jax import lax
from jax.experimental import pallas as pl
from jax.experimental.pallas import tpu as pltpu
from jax.sharding import PartitionSpec as P

LEVELS = 4
RADIUS = 2
SLOTS = 4
TR = 8
TC = 128
PIX = TR * TC
CIN = 128
CH = 256
POOLED = PIX // 4 + PIX // 16 + PIX // 64
PAD = 384
CELLS = PIX + PAD
CHUNK = 256
LIMIT = 193 << 18
WIN = 2 * RADIUS * TR + TR + 2

NN = (((1,), (0,)), ((), ()))
NT = (((1,), (1,)), ((), ()))
TN = (((0,), (0,)), ((), ()))


def matmul(a, b, dims):
    return lax.dot_general(a, b, dims, preferred_element_type=jnp.float32)


def routes(count):
    side = [1 - 2 * (i % 2) for i in range(count)]

    def keep(pairs):
        return [(a, b) for a, b in pairs if 0 <= b < count]

    return dict(
        swap=[(i, i + side[i]) for i in range(count)],
        ahead=keep((i, i + 2 * side[i]) for i in range(count)),
        behind=keep((i, i - 2 * side[i]) for i in range(count)),
        far=keep((i, i - 3 * side[i]) for i in range(count)),
        cross=keep((i, i - side[i]) for i in range(count)),
    )


def shifted(block):
    n = block.shape[0]
    column = lax.broadcasted_iota(jnp.int32, block.shape, 0)
    down = jnp.where(column == 0, 0.0, pltpu.roll(block, 1, 0))
    up = jnp.where(column == n - 1, 0.0, pltpu.roll(block, n - 1, 0))
    return down, up


def spread_columns(source, row, target, at):
    middle = source[row]
    down, up = shifted(middle.astype(jnp.float32))
    where = pl.ds(pl.multiple_of(at * TC, TC), TC)
    target[where, 0:CIN] = down.astype(jnp.bfloat16)
    target[where, CIN : 2 * CIN] = middle
    target[where, 2 * CIN : 3 * CIN] = up.astype(jnp.bfloat16)


def convolve(spread, at, weight):
    parts = [
        spread[pl.ds(pl.multiple_of((at + a) * TC, TC), PIX), :] for a in range(3)
    ]
    total = matmul(jnp.concatenate(parts, 1), weight[...], NN)
    return total.astype(jnp.bfloat16)


def spread_back(gradient, moved):
    for r in range(TR):
        rows = slice(r * TC, (r + 1) * TC)
        block = gradient[rows, :]
        down, up = shifted(block)
        moved[rows, 0:CH] = up.astype(jnp.bfloat16)
        moved[rows, CH : 2 * CH] = block.astype(jnp.bfloat16)
        moved[rows, 2 * CH : 3 * CH] = down.astype(jnp.bfloat16)


def convolve_back(moved, weight_back, total, at):
    parts = matmul(moved[...], weight_back[...], NT)
    for a in range(3):
        where = pl.ds(pl.multiple_of((at + a) * TC, TC), PIX)
        total[where, :] += parts[:, a * CIN : (a + 1) * CIN]


def pool_matrix(shape, cell_axis, values):
    cell = lax.broadcasted_iota(jnp.int32, shape, cell_axis)
    pixel = lax.broadcasted_iota(jnp.int32, shape, 1 - cell_axis)
    row, column = pixel // TC, pixel % TC
    offset = 0
    result = jnp.zeros(shape, jnp.float32)
    for level in range(1, LEVELS):
        own = offset + (row >> level) * (TC >> level) + (column >> level)
        result = jnp.where(cell == own, values[level], result)
        offset += PIX >> (2 * level)
    return result.astype(jnp.bfloat16)


def per_level(values, fill):
    cell = lax.broadcasted_iota(jnp.int32, (PAD, 1), 0)
    result = jnp.full((PAD, 1), fill, jnp.float32)
    offset = 0
    for level in range(1, LEVELS):
        result = jnp.where(cell >= offset, values[level], result)
        offset += PIX >> (2 * level)
    return jnp.where(cell >= offset, fill, result)


def tile_side():
    return 1 - 2 * lax.rem(lax.axis_index("tile"), 2)


def tables_kernel(pool, unpool):
    pool[...] = pool_matrix((PAD, PIX), 0, [1.0] * LEVELS)
    unpool[...] = pool_matrix((PIX, PAD), 1, [2.0**-level for level in range(LEVELS)])


def rows_kernel(one, two, cross, far, inward, sems):
    side = tile_side()
    facing = jnp.where(side > 0, TR - 1, 0)
    outer = jnp.where(side > 0, 0, TR - 1)
    copies = [
        pltpu.make_async_copy(one.at[pl.ds(outer, 1)], cross, sems.at[0]),
        pltpu.make_async_copy(two.at[pl.ds(outer, 1)], far, sems.at[1]),
        pltpu.make_async_copy(one.at[pl.ds(facing, 1)], inward, sems.at[2]),
    ]
    for copy in copies:
        copy.start()
    for copy in copies:
        copy.wait()


def write_labels(targets, labels):
    value = targets[...]
    inside = value % PIX
    row, column = inside // TC, inside % TC
    offset = 0
    for level in range(LEVELS):
        cells = offset + (row >> level) * (TC >> level) + (column >> level)
        for r in range(TR):
            labels[level : level + 1, r * TC : (r + 1) * TC] = cells[r : r + 1, :]
        offset += PIX >> (2 * level)
    slots = value // PIX
    for r in range(TR):
        labels[LEVELS : LEVELS + 1, r * TC : (r + 1) * TC] = slots[r : r + 1, :]


def work_kernel(
    partners,
    counts,
    own_one,
    own_two,
    near,
    direct,
    far,
    cross,
    from_sibling,
    weight,
    pool,
    unpool,
    targets,
    to_sibling_hbm,
    ahead_hbm,
    behind_hbm,
    far_hbm,
    sum_one_hbm,
    sum_two_hbm,
    to_sibling,
    ahead,
    behind,
    far_out,
    sum_one,
    sum_two,
    sems,
    move_sems,
    weight_back,
    labels,
    window,
    spread_two,
    window_one,
    spread_one,
    feat_one,
    feat_two,
    pyramid,
    dscore,
    level_grad,
    grad_rows,
    moved,
    total_two,
    total_one,
):
    index = lax.axis_index("tile")
    side = tile_side()
    count = counts[0]

    def at(offset):
        return 1 + TR * (offset + RADIUS)

    def edge(sign):
        return jnp.where(sign > 0, WIN - 1, 0)

    def block(row):
        return window.at[pl.ds(row, TR)]

    def single(target, row):
        return target.at[pl.ds(row, 1)]

    def arrived(first, size=1):
        return from_sibling.at[pl.ds(first, size)]

    moves = [
        (own_two, block(at(0))),
        (near, block(at(2 * side))),
        (direct, block(at(-2 * side))),
        (arrived(0, TR), block(at(side))),
        (arrived(TR, TR), block(at(-side))),
        (arrived(2 * TR + 1), single(window, edge(side))),
        (far, single(window, edge(-side))),
        (own_one, window_one.at[pl.ds(1, TR)]),
        (arrived(2 * TR), single(window_one, jnp.where(side > 0, TR + 1, 0))),
        (cross, single(window_one, jnp.where(side > 0, 0, TR + 1))),
    ]
    moves = [
        pltpu.make_async_copy(source, target, move_sems.at[n])
        for n, (source, target) in enumerate(moves)
    ]
    for move in moves:
        move.start()
    write_labels(targets, labels)

    for a in range(3):
        for b in range(3):
            weight_back[a * CIN : (a + 1) * CIN, b * CH : (b + 1) * CH] = weight[
                (3 * a + b) * CIN : (3 * a + b + 1) * CIN, :
            ]

    grad_rows[...] = jnp.zeros_like(grad_rows)
    total_two[...] = jnp.zeros_like(total_two)
    total_one[...] = jnp.zeros_like(total_one)
    for move in moves:
        move.wait()

    def spread(r, carry):
        spread_columns(window, r, spread_two, r)
        return carry

    lax.fori_loop(0, WIN, spread, 0)
    for r in range(TR + 2):
        spread_columns(window_one, r, spread_one, r)
    feat_one[...] = convolve(spread_one, 0, weight)

    def first_row(k):
        return TR * (partners[0, k] - index + RADIUS)

    feat_two[...] = convolve(spread_two, first_row(0), weight)

    def work_slot(k):
        features = feat_one[...]
        here = labels[LEVELS : LEVELS + 1, :] == k
        columns = [jnp.where(here, labels[m : m + 1, :], -1) for m in range(LEVELS)]

        def score(start, size, hits):
            half_score = matmul(pyramid[start : start + size, :], features, NT)
            position = lax.broadcasted_iota(jnp.int32, half_score.shape, 0) + start
            hit = position == hits[0]
            for more in hits[1:]:
                hit = hit | (position == more)
            value = jnp.tanh(half_score - 1.0) + jnp.where(hit, -1.0, 1.0)
            dscore[start : start + size, :] = value.astype(jnp.bfloat16)

        pyramid[0:PIX, :] = feat_two[...] * jnp.bfloat16(2.0**-5)
        score(0, CHUNK, columns[:1])
        means = matmul(pool[...], feat_two[...], NN) * per_level(
            [4.0**-level for level in range(LEVELS)], 0.0
        )
        scale = per_level([2.0 ** (level - 5) for level in range(LEVELS)], 0.0)
        pyramid[PIX:CELLS, :] = (
            means.astype(jnp.bfloat16).astype(jnp.float32) * scale
        ).astype(jnp.bfloat16)
        for start in range(CHUNK, PIX, CHUNK):
            score(start, CHUNK, columns[:1])
        score(PIX, PIX // 4, columns[1:2])
        score(PIX + PIX // 4, PAD - PIX // 4, columns[2:])
        level_grad[PIX:CELLS, :] = matmul(dscore[PIX:CELLS, :], features, NN)
        level_grad[0:PIX, :] = matmul(dscore[0:PIX, :], features, NN)
        coarse = level_grad[PIX:CELLS, :].astype(jnp.bfloat16)
        gradient = level_grad[0:PIX, :] + matmul(unpool[...], coarse, NN)
        level_grad[0:PIX, :] = gradient * 2.0**-5
        spread_back(level_grad, moved)
        feat_two[...] = convolve(spread_two, first_row(jnp.minimum(k + 1, SLOTS - 1)), weight)
        grad_rows[...] += matmul(dscore[...], pyramid[...], TN)
        convolve_back(moved, weight_back, total_two, first_row(k))

    def slot(k, carry):
        pl.when(k < count)(lambda: work_slot(k))
        return carry

    lax.fori_loop(0, SLOTS, slot, 0)

    def rows(total, row, size=1):
        return total[pl.ds(pl.multiple_of(row * TC, TC), size * TC), :].reshape(size, TC, CIN)

    def out(n, block, target):
        return pltpu.make_async_copy(block, target, sems.at[n])

    behind[...] = rows(total_two, at(-2 * side), TR)
    out(0, behind, behind_hbm).start()
    far_out[...] = rows(total_two, edge(-side)).astype(jnp.bfloat16)
    out(1, far_out, far_hbm).start()
    ahead[...] = rows(total_two, at(2 * side), TR)
    out(2, ahead, ahead_hbm).start()
    sum_two[...] = rows(total_two, at(0), TR)
    out(3, sum_two, sum_two_hbm).start()
    to_sibling[0:TR] = rows(total_two, at(side), TR).astype(jnp.bfloat16)
    to_sibling[TR : 2 * TR] = rows(total_two, at(-side), TR).astype(jnp.bfloat16)
    to_sibling[2 * TR : 2 * TR + 1] = rows(total_two, edge(side)).astype(jnp.bfloat16)
    spread_back(grad_rows, moved)
    convolve_back(moved, weight_back, total_one, 0)
    facing = jnp.where(side > 0, TR + 1, 0)
    outer = jnp.where(side > 0, 0, TR + 1)
    to_sibling[2 * TR + 1 : 2 * TR + 2] = rows(total_one, facing).astype(jnp.bfloat16)
    to_sibling[2 * TR + 2 : 2 * TR + 3] = rows(total_one, outer).astype(jnp.bfloat16)
    out(4, to_sibling, to_sibling_hbm).start()
    sum_one[...] = rows(total_one, 1, TR)
    out(5, sum_one, sum_one_hbm).start()
    out(0, behind, behind_hbm).wait()
    out(1, far_out, far_hbm).wait()
    out(2, ahead, ahead_hbm).wait()
    out(3, sum_two, sum_two_hbm).wait()
    out(4, to_sibling, to_sibling_hbm).wait()
    out(5, sum_one, sum_one_hbm).wait()


def call(kernel, outs, scratch, args, name, in_spaces, out_spaces):
    return pl.pallas_call(
        kernel,
        in_specs=[pl.BlockSpec(memory_space=space) for space in in_spaces],
        out_specs=[pl.BlockSpec(memory_space=space) for space in out_spaces],
        out_shape=[jax.ShapeDtypeStruct(*out) for out in outs],
        scratch_shapes=scratch,
        compiler_params=pltpu.CompilerParams(vmem_limit_bytes=LIMIT),
        name=name,
    )(*args)


def on_device(frame_one, frame_two, conv_weight, partners, counts, targets):
    route = routes(lax.axis_size("tile"))
    index = lax.axis_index("tile")
    side = 1 - 2 * (index % 2)
    f32, bf16 = jnp.float32, jnp.bfloat16

    def send(block, name):
        return lax.ppermute(block, "tile", route[name])

    row_block = (1, TC, CIN)
    frames = [
        pltpu.with_memory_space_constraint(frame, pltpu.HBM) for frame in (frame_one, frame_two)
    ]
    weight = conv_weight.reshape(9 * CIN, CH)
    direct = send(frame_two, "ahead")
    near = send(frame_two, "behind")
    cross_in, far_in, inward = call(
        rows_kernel,
        [(row_block, bf16)] * 3,
        [pltpu.SemaphoreType.DMA((3,))],
        frames,
        "rows",
        [pltpu.HBM] * 2,
        [pltpu.HBM] * 3,
    )
    far = send(far_in, "far")
    cross = send(cross_in, "cross")
    pool, unpool = call(
        tables_kernel,
        [((PAD, PIX), bf16), ((PIX, PAD), bf16)],
        [],
        [],
        "tables",
        [],
        [pltpu.VMEM] * 2,
    )
    inward, far, cross, pool, unpool = lax.optimization_barrier(
        (inward, far, cross, pool, unpool)
    )
    facing_row = jnp.where(side > 0, TR - 1, 0)
    direct_row = lax.dynamic_slice_in_dim(direct, facing_row, 1, 0)
    payload = jnp.concatenate([frame_two, near, inward, direct_row])
    from_sibling = send(payload, "swap")

    tile = (TR, TC, CIN)
    pack = (2 * TR + 3, TC, CIN)
    outs = [
        (pack, bf16),
        (tile, f32),
        (tile, f32),
        ((1, TC, CIN), bf16),
        (tile, f32),
        (tile, f32),
    ]
    scratch = [
        ((3 * CIN, 3 * CH), bf16),
        ((8, PIX), jnp.int32),
        ((WIN, TC, CIN), bf16),
        ((WIN * TC, 3 * CIN), bf16),
        ((TR + 2, TC, CIN), bf16),
        (((TR + 2) * TC, 3 * CIN), bf16),
        ((PIX, CH), bf16),
        ((PIX, CH), bf16),
        ((CELLS, CH), bf16),
        ((CELLS, PIX), bf16),
        ((CELLS, CH), f32),
        ((PIX, CH), f32),
        ((PIX, 3 * CH), bf16),
        ((WIN * TC, CIN), f32),
        (((TR + 2) * TC, CIN), f32),
    ]
    to_sibling, ahead, behind, far_out, sum_one, sum_two = call(
        work_kernel,
        outs,
        [pltpu.VMEM(*out) for out in outs]
        + [pltpu.SemaphoreType.DMA((len(outs),)), pltpu.SemaphoreType.DMA((10,))]
        + [pltpu.VMEM(*item) for item in scratch],
        [partners, counts, *frames, near, direct, far, cross]
        + [from_sibling, weight, pool, unpool, targets],
        "work",
        [pltpu.SMEM] * 2 + [pl.ANY] * 7 + [pltpu.VMEM] * 4,
        [pltpu.HBM] * len(outs),
    )
    row = lax.broadcasted_iota(jnp.int32, (TR, 1, 1), 0)
    facing = row == jnp.where(side > 0, TR - 1, 0)
    outer = row == jnp.where(side > 0, 0, TR - 1)
    back_sibling = send(to_sibling, "swap")
    ahead_in = (ahead + back_sibling[TR : 2 * TR].astype(f32)).astype(bf16)
    edge = jnp.where(facing, back_sibling[2 * TR : 2 * TR + 1].astype(f32), 0.0)
    behind_in = (behind + edge).astype(bf16)
    back_ahead = send(jnp.concatenate([ahead_in, back_sibling[2 * TR + 2 :]]), "ahead")
    back_behind = send(behind_in, "behind")
    back_far = send(far_out, "far")

    def place(where, block):
        return jnp.where(where, block.astype(f32), 0.0)

    grad_one = sum_one + place(facing, back_sibling[2 * TR + 1 : 2 * TR + 2])
    grad_one = grad_one + place(outer, back_ahead[TR:])
    grad_two = sum_two + back_sibling[:TR].astype(f32) + back_ahead[:TR].astype(f32)
    grad_two = grad_two + back_behind.astype(f32)
    grad_two = grad_two + place(outer, back_far)
    return grad_one.astype(bf16), grad_two.astype(bf16)


def solution(mesh):
    return jax.shard_map(
        on_device,
        mesh=mesh,
        in_specs=(
            P(("groups", "tile"), None, None),
            P(("groups", "tile"), None, None),
            P(),
            P(("groups", "tile"), None),
            P(("groups", "tile")),
            P(("groups", "tile"), None),
        ),
        out_specs=(P(("groups", "tile"), None, None), P(("groups", "tile"), None, None)),
        check_vma=False,
    )
```

```python
import functools

import jax
import jax.numpy as jnp
import numpy as np
from jax import lax
from jax.experimental import pallas as pl
from jax.experimental.pallas import tpu as pltpu
from jax.sharding import PartitionSpec as P

LEVELS = 4
RADIUS = 2
SLOTS = 4
TR = 8
TC = 128
PIX = TR * TC
CIN = 128
CH = 256
POOLED = PIX // 4 + PIX // 16 + PIX // 64
PAD = 384
CELLS = PIX + PAD
CHUNK = 256
LIMIT = 193 << 18
WIN = 2 * RADIUS * TR + TR + 2

NN = (((1,), (0,)), ((), ()))
NT = (((1,), (1,)), ((), ()))
TN = (((0,), (0,)), ((), ()))


def matmul(a, b, dims):
    return lax.dot_general(a, b, dims, preferred_element_type=jnp.float32)


def routes(count):
    side = [1 - 2 * (i % 2) for i in range(count)]

    def keep(pairs):
        return [(a, b) for a, b in pairs if 0 <= b < count]

    return dict(
        swap=[(i, i + side[i]) for i in range(count)],
        ahead=keep((i, i + 2 * side[i]) for i in range(count)),
        behind=keep((i, i - 2 * side[i]) for i in range(count)),
        far=keep((i, i - 3 * side[i]) for i in range(count)),
        cross=keep((i, i - side[i]) for i in range(count)),
    )


def shifted(block):
    n = block.shape[0]
    column = lax.broadcasted_iota(jnp.int32, block.shape, 0)
    down = jnp.where(column == 0, 0.0, pltpu.roll(block, 1, 0))
    up = jnp.where(column == n - 1, 0.0, pltpu.roll(block, n - 1, 0))
    return down, up


def spread_columns(source, row, target, at):
    middle = source[row]
    down, up = shifted(middle.astype(jnp.float32))
    where = pl.ds(pl.multiple_of(at * TC, TC), TC)
    target[where, 0:CIN] = down.astype(jnp.bfloat16)
    target[where, CIN : 2 * CIN] = middle
    target[where, 2 * CIN : 3 * CIN] = up.astype(jnp.bfloat16)


def convolve(spread, at, weight):
    parts = [
        spread[pl.ds(pl.multiple_of((at + a) * TC, TC), PIX), :] for a in range(3)
    ]
    total = matmul(jnp.concatenate(parts, 1), weight[...], NN)
    return total.astype(jnp.bfloat16)


def spread_back(gradient, moved):
    for r in range(TR):
        rows = slice(r * TC, (r + 1) * TC)
        block = gradient[rows, :]
        down, up = shifted(block)
        moved[rows, 0:CH] = up.astype(jnp.bfloat16)
        moved[rows, CH : 2 * CH] = block.astype(jnp.bfloat16)
        moved[rows, 2 * CH : 3 * CH] = down.astype(jnp.bfloat16)


def convolve_back(moved, weight_back, total, at):
    parts = matmul(moved[...], weight_back[...], NT)
    for a in range(3):
        where = pl.ds(pl.multiple_of((at + a) * TC, TC), PIX)
        total[where, :] += parts[:, a * CIN : (a + 1) * CIN]


def pool_matrix(shape, cell_axis, values):
    cell = lax.broadcasted_iota(jnp.int32, shape, cell_axis)
    pixel = lax.broadcasted_iota(jnp.int32, shape, 1 - cell_axis)
    row, column = pixel // TC, pixel % TC
    offset = 0
    result = jnp.zeros(shape, jnp.float32)
    for level in range(1, LEVELS):
        own = offset + (row >> level) * (TC >> level) + (column >> level)
        result = jnp.where(cell == own, values[level], result)
        offset += PIX >> (2 * level)
    return result.astype(jnp.bfloat16)


def per_level(values, fill):
    cell = lax.broadcasted_iota(jnp.int32, (PAD, 1), 0)
    result = jnp.full((PAD, 1), fill, jnp.float32)
    offset = 0
    for level in range(1, LEVELS):
        result = jnp.where(cell >= offset, values[level], result)
        offset += PIX >> (2 * level)
    return jnp.where(cell >= offset, fill, result)


def tile_side():
    return 1 - 2 * lax.rem(lax.axis_index("tile"), 2)


def tables_kernel(pool, unpool):
    pool[...] = pool_matrix((PAD, PIX), 0, [1.0] * LEVELS)
    unpool[...] = pool_matrix((PIX, PAD), 1, [2.0**-level for level in range(LEVELS)])


def rows_kernel(one, two, cross, far, inward, sems):
    side = tile_side()
    facing = jnp.where(side > 0, TR - 1, 0)
    outer = jnp.where(side > 0, 0, TR - 1)
    copies = [
        pltpu.make_async_copy(one.at[pl.ds(outer, 1)], cross, sems.at[0]),
        pltpu.make_async_copy(two.at[pl.ds(outer, 1)], far, sems.at[1]),
        pltpu.make_async_copy(one.at[pl.ds(facing, 1)], inward, sems.at[2]),
    ]
    for copy in copies:
        copy.start()
    for copy in copies:
        copy.wait()


def write_labels(targets, labels):
    value = targets[...]
    inside = value % PIX
    row, column = inside // TC, inside % TC
    offset = 0
    for level in range(LEVELS):
        cells = offset + (row >> level) * (TC >> level) + (column >> level)
        for r in range(TR):
            labels[level : level + 1, r * TC : (r + 1) * TC] = cells[r : r + 1, :]
        offset += PIX >> (2 * level)
    slots = value // PIX
    for r in range(TR):
        labels[LEVELS : LEVELS + 1, r * TC : (r + 1) * TC] = slots[r : r + 1, :]


def work_kernel(
    partners,
    counts,
    own_one,
    own_two,
    near,
    direct,
    far,
    cross,
    from_sibling,
    weight,
    pool,
    unpool,
    targets,
    to_sibling_hbm,
    ahead_hbm,
    behind_hbm,
    far_hbm,
    edge_hbm,
    sum_one_hbm,
    sum_two_hbm,
    to_sibling,
    ahead,
    behind,
    far_out,
    edge_out,
    sum_one,
    sum_two,
    sems,
    move_sems,
    weight_back,
    labels,
    window,
    spread_two,
    window_one,
    spread_one,
    feat_one,
    feat_two,
    pyramid,
    dscore,
    level_grad,
    grad_rows,
    moved,
    total_two,
    total_one,
):
    index = lax.axis_index("tile")
    side = tile_side()
    count = counts[0]

    def at(offset):
        return 1 + TR * (offset + RADIUS)

    def edge(sign):
        return jnp.where(sign > 0, WIN - 1, 0)

    def block(row):
        return window.at[pl.ds(row, TR)]

    def single(target, row):
        return target.at[pl.ds(row, 1)]

    def arrived(first, size=1):
        return from_sibling.at[pl.ds(first, size)]

    moves = [
        (own_two, block(at(0))),
        (near, block(at(2 * side))),
        (direct, block(at(-2 * side))),
        (arrived(0, TR), block(at(side))),
        (arrived(TR, TR), block(at(-side))),
        (arrived(2 * TR + 1), single(window, edge(side))),
        (far, single(window, edge(-side))),
        (own_one, window_one.at[pl.ds(1, TR)]),
        (arrived(2 * TR), single(window_one, jnp.where(side > 0, TR + 1, 0))),
        (cross, single(window_one, jnp.where(side > 0, 0, TR + 1))),
    ]
    moves = [
        pltpu.make_async_copy(source, target, move_sems.at[n])
        for n, (source, target) in enumerate(moves)
    ]
    for move in moves:
        move.start()
    write_labels(targets, labels)

    for a in range(3):
        for b in range(3):
            weight_back[a * CIN : (a + 1) * CIN, b * CH : (b + 1) * CH] = weight[
                (3 * a + b) * CIN : (3 * a + b + 1) * CIN, :
            ]

    grad_rows[...] = jnp.zeros_like(grad_rows)
    total_two[...] = jnp.zeros_like(total_two)
    total_one[...] = jnp.zeros_like(total_one)
    for move in moves:
        move.wait()

    def spread(r, carry):
        spread_columns(window, r, spread_two, r)
        return carry

    lax.fori_loop(0, WIN, spread, 0)
    for r in range(TR + 2):
        spread_columns(window_one, r, spread_one, r)
    feat_one[...] = convolve(spread_one, 0, weight)

    def first_row(k):
        return TR * (partners[0, k] - index + RADIUS)

    feat_two[...] = convolve(spread_two, first_row(0), weight)

    def work_slot(k):
        features = feat_one[...]
        here = labels[LEVELS : LEVELS + 1, :] == k
        columns = [jnp.where(here, labels[m : m + 1, :], -1) for m in range(LEVELS)]

        def score(start, size, hits):
            half_score = matmul(pyramid[start : start + size, :], features, NT)
            position = lax.broadcasted_iota(jnp.int32, half_score.shape, 0) + start
            hit = position == hits[0]
            for more in hits[1:]:
                hit = hit | (position == more)
            value = jnp.tanh(half_score - 1.0) + jnp.where(hit, -1.0, 1.0)
            dscore[start : start + size, :] = value.astype(jnp.bfloat16)

        pyramid[0:PIX, :] = feat_two[...] * jnp.bfloat16(2.0**-5)
        score(0, CHUNK, columns[:1])
        means = matmul(pool[...], feat_two[...], NN) * per_level(
            [4.0**-level for level in range(LEVELS)], 0.0
        )
        scale = per_level([2.0 ** (level - 5) for level in range(LEVELS)], 0.0)
        pyramid[PIX:CELLS, :] = (
            means.astype(jnp.bfloat16).astype(jnp.float32) * scale
        ).astype(jnp.bfloat16)
        for start in range(CHUNK, PIX, CHUNK):
            score(start, CHUNK, columns[:1])
        score(PIX, PIX // 4, columns[1:2])
        score(PIX + PIX // 4, PAD - PIX // 4, columns[2:])
        level_grad[PIX:CELLS, :] = matmul(dscore[PIX:CELLS, :], features, NN)
        level_grad[0:PIX, :] = matmul(dscore[0:PIX, :], features, NN)
        coarse = level_grad[PIX:CELLS, :].astype(jnp.bfloat16)
        gradient = level_grad[0:PIX, :] + matmul(unpool[...], coarse, NN)
        level_grad[0:PIX, :] = gradient * 2.0**-5
        spread_back(level_grad, moved)
        feat_two[...] = convolve(spread_two, first_row(jnp.minimum(k + 1, SLOTS - 1)), weight)
        grad_rows[...] += matmul(dscore[...], pyramid[...], TN)
        convolve_back(moved, weight_back, total_two, first_row(k))

    def slot(k, carry):
        pl.when(k < count)(lambda: work_slot(k))
        return carry

    lax.fori_loop(0, SLOTS, slot, 0)

    def rows(total, row, size=1):
        return total[pl.ds(pl.multiple_of(row * TC, TC), size * TC), :].reshape(size, TC, CIN)

    def out(n, block, target):
        return pltpu.make_async_copy(block, target, sems.at[n])

    behind[...] = rows(total_two, at(-2 * side), TR).astype(jnp.bfloat16)
    out(0, behind, behind_hbm).start()
    far_out[...] = rows(total_two, edge(-side)).astype(jnp.bfloat16)
    out(1, far_out, far_hbm).start()
    edge_out[...] = rows(total_two, edge(side)).astype(jnp.bfloat16)
    out(6, edge_out, edge_hbm).start()
    ahead[...] = rows(total_two, at(2 * side), TR)
    out(2, ahead, ahead_hbm).start()
    sum_two[...] = rows(total_two, at(0), TR)
    out(3, sum_two, sum_two_hbm).start()
    to_sibling[0:TR] = rows(total_two, at(side), TR).astype(jnp.bfloat16)
    to_sibling[TR : 2 * TR] = rows(total_two, at(-side), TR).astype(jnp.bfloat16)
    spread_back(grad_rows, moved)
    convolve_back(moved, weight_back, total_one, 0)
    facing = jnp.where(side > 0, TR + 1, 0)
    outer = jnp.where(side > 0, 0, TR + 1)
    to_sibling[2 * TR : 2 * TR + 1] = rows(total_one, facing).astype(jnp.bfloat16)
    to_sibling[2 * TR + 1 : 2 * TR + 2] = rows(total_one, outer).astype(jnp.bfloat16)
    out(4, to_sibling, to_sibling_hbm).start()
    sum_one[...] = rows(total_one, 1, TR)
    out(5, sum_one, sum_one_hbm).start()
    out(0, behind, behind_hbm).wait()
    out(1, far_out, far_hbm).wait()
    out(6, edge_out, edge_hbm).wait()
    out(2, ahead, ahead_hbm).wait()
    out(3, sum_two, sum_two_hbm).wait()
    out(4, to_sibling, to_sibling_hbm).wait()
    out(5, sum_one, sum_one_hbm).wait()


def call(kernel, outs, scratch, args, name, in_spaces, out_spaces):
    return pl.pallas_call(
        kernel,
        in_specs=[pl.BlockSpec(memory_space=space) for space in in_spaces],
        out_specs=[pl.BlockSpec(memory_space=space) for space in out_spaces],
        out_shape=[jax.ShapeDtypeStruct(*out) for out in outs],
        scratch_shapes=scratch,
        compiler_params=pltpu.CompilerParams(vmem_limit_bytes=LIMIT),
        name=name,
    )(*args)


def on_device(frame_one, frame_two, conv_weight, partners, counts, targets):
    route = routes(lax.axis_size("tile"))
    index = lax.axis_index("tile")
    side = 1 - 2 * (index % 2)
    f32, bf16 = jnp.float32, jnp.bfloat16

    def send(block, name):
        return lax.ppermute(block, "tile", route[name])

    row_block = (1, TC, CIN)
    frames = [
        pltpu.with_memory_space_constraint(frame, pltpu.HBM) for frame in (frame_one, frame_two)
    ]
    weight = conv_weight.reshape(9 * CIN, CH)
    direct = send(frame_two, "ahead")
    near = send(frame_two, "behind")
    cross_in, far_in, inward = call(
        rows_kernel,
        [(row_block, bf16)] * 3,
        [pltpu.SemaphoreType.DMA((3,))],
        frames,
        "rows",
        [pltpu.HBM] * 2,
        [pltpu.HBM] * 3,
    )
    far = send(far_in, "far")
    cross = send(cross_in, "cross")
    pool, unpool = call(
        tables_kernel,
        [((PAD, PIX), bf16), ((PIX, PAD), bf16)],
        [],
        [],
        "tables",
        [],
        [pltpu.VMEM] * 2,
    )
    inward, far, cross, pool, unpool = lax.optimization_barrier(
        (inward, far, cross, pool, unpool)
    )
    facing_row = jnp.where(side > 0, TR - 1, 0)
    direct_row = lax.dynamic_slice_in_dim(direct, facing_row, 1, 0)
    payload = jnp.concatenate([frame_two, near, inward, direct_row])
    from_sibling = send(payload, "swap")

    tile = (TR, TC, CIN)
    pack = (2 * TR + 2, TC, CIN)
    outs = [
        (pack, bf16),
        (tile, f32),
        (tile, bf16),
        ((1, TC, CIN), bf16),
        ((1, TC, CIN), bf16),
        (tile, f32),
        (tile, f32),
    ]
    scratch = [
        ((3 * CIN, 3 * CH), bf16),
        ((8, PIX), jnp.int32),
        ((WIN, TC, CIN), bf16),
        ((WIN * TC, 3 * CIN), bf16),
        ((TR + 2, TC, CIN), bf16),
        (((TR + 2) * TC, 3 * CIN), bf16),
        ((PIX, CH), bf16),
        ((PIX, CH), bf16),
        ((CELLS, CH), bf16),
        ((CELLS, PIX), bf16),
        ((CELLS, CH), f32),
        ((PIX, CH), f32),
        ((PIX, 3 * CH), bf16),
        ((WIN * TC, CIN), f32),
        (((TR + 2) * TC, CIN), f32),
    ]
    to_sibling, ahead, behind, far_out, edge, sum_one, sum_two = call(
        work_kernel,
        outs,
        [pltpu.VMEM(*out) for out in outs]
        + [pltpu.SemaphoreType.DMA((len(outs),)), pltpu.SemaphoreType.DMA((10,))]
        + [pltpu.VMEM(*item) for item in scratch],
        [partners, counts, *frames, near, direct, far, cross]
        + [from_sibling, weight, pool, unpool, targets],
        "work",
        [pltpu.SMEM] * 2 + [pl.ANY] * 7 + [pltpu.VMEM] * 4,
        [pltpu.HBM] * len(outs),
    )
    row = lax.broadcasted_iota(jnp.int32, (TR, 1, 1), 0)
    facing = row == jnp.where(side > 0, TR - 1, 0)
    outer = row == jnp.where(side > 0, 0, TR - 1)
    back_sibling = send(to_sibling, "swap")
    ahead_in = (ahead + back_sibling[TR : 2 * TR].astype(f32)).astype(bf16)
    back_behind = send(behind, "behind")
    ahead_in = jnp.concatenate([ahead_in, back_sibling[2 * TR + 1 :], edge])
    back_ahead = send(ahead_in, "ahead")
    back_edge = send(back_ahead[TR + 1 :], "swap")
    back_far = send(far_out, "far")

    def place(where, block):
        return jnp.where(where, block.astype(f32), 0.0)

    grad_one = sum_one + place(facing, back_sibling[2 * TR : 2 * TR + 1])
    grad_one = grad_one + place(outer, back_ahead[TR : TR + 1])
    grad_two = sum_two + back_sibling[:TR].astype(f32) + back_ahead[:TR].astype(f32)
    grad_two = grad_two + back_behind.astype(f32)
    grad_two = grad_two + place(outer, back_far) + place(facing, back_edge)
    return grad_one.astype(bf16), grad_two.astype(bf16)


def solution(mesh):
    return jax.shard_map(
        on_device,
        mesh=mesh,
        in_specs=(
            P(("groups", "tile"), None, None),
            P(("groups", "tile"), None, None),
            P(),
            P(("groups", "tile"), None),
            P(("groups", "tile")),
            P(("groups", "tile"), None),
        ),
        out_specs=(P(("groups", "tile"), None, None), P(("groups", "tile"), None, None)),
        check_vma=False,
    )
```
